512 devices in a mesh: chan: 16 (over z, x_lo), tm: 32 (over y, x_hi, core).
Axes of the slice: x: 4 (x_hi: 2, x_lo: 2; x = x_hi * 2 + x_lo), y: 8, z: 8, core: 2. Of those that a mesh axis runs over, the one named last changes fastest.
Arguments:
- strain_rate: float32 [4096, 16384], P('chan', 'tm'), may hold values from -64 to 64
Outputs:
- stacks: float32 [128, 8, 13056], P('chan', None, 'tm')
The draws below stay inside these ranges and needn't reach their ends.
All inputs are finite; a program needn't handle non-finite values.
Results may differ from the reference program's by a relative error of at most 0.0041.
Values may be sent and summed in bfloat16 or wider, within the bound.
A program may use at most 64 MiB of HBM per device.

```python
import math
import jax
import jax.numpy as jnp
from jax import lax

CB = 256
SRC = 8
TS = 512
MAXLAG = 25
W2 = 64
LAGS = 51
N_CHAN = 16
N_TM = 32


def draw_strain_rate(key, part):
    key_chan, key_seg, key_noise = jax.random.split(key, 3)
    channels = CB * N_CHAN
    samples = TS * N_TM
    chan_gain = jnp.exp(jax.random.uniform(key_chan, (channels, 1), jnp.float32, 0.0, math.log(4.0)))
    seg_gain = jnp.exp(jax.random.uniform(key_seg, (channels, samples // 32), jnp.float32, math.log(0.5), math.log(4.0)))
    noise = jax.random.truncated_normal(key_noise, -4.0, 4.0, (channels, samples), jnp.float32)
    seg_gain = jnp.repeat(seg_gain, 32, axis=1)
    return (noise * chan_gain * seg_gain).astype(jnp.float32)


def setup_inputs(seed: int = 0) -> dict:
    keys = jax.random.split(jax.random.key(seed), 2)
    strain_rate = draw_strain_rate(jax.random.fold_in(keys[1], 71), 0)
    return {"strain_rate": strain_rate}


def running_level(strain_rate):
    magnitude = jnp.abs(strain_rate)
    window_sums = lax.reduce_window(magnitude, jnp.zeros((), magnitude.dtype), lax.add, (1, 2 * W2 + 1), (1, 1), ((0, 0), (W2, W2)))
    return window_sums / (2 * W2 + 1) + 1e-05

def lag_sources(source_shards):
    padded = jnp.pad(source_shards, ((0, 0), (0, 0), (MAXLAG, MAXLAG)))
    windows = [padded[:, :, 2 * MAXLAG - position:2 * MAXLAG - position + TS] for position in range(LAGS)]
    return jnp.stack(windows, axis=1)

def block_stack(source_rows, receivers):
    source_shards = source_rows.reshape(SRC, N_TM, TS).astype(jnp.float32)
    receiver_shards = receivers.reshape(CB, N_TM, TS).astype(jnp.float32)
    lagged = lag_sources(source_shards)
    product = jnp.einsum('slku,bku->ksbl', lagged, receiver_shards)
    partial_value = product * (1.0 / math.sqrt(TS * N_TM))
    return lax.optimization_barrier(jnp.sum(partial_value, axis=0)).reshape(SRC, CB * LAGS)

def reference(strain_rate):
    normed = (strain_rate / running_level(strain_rate)).astype(jnp.bfloat16)
    blocks = normed.reshape(N_CHAN, CB, TS * N_TM)
    sources = blocks[:, ::CB // SRC, :]
    reach_steps = N_CHAN // 4
    offsets = list(range(-reach_steps, 0)) + list(range(1, reach_steps + 1))
    per_offset = []
    for offset in offsets:
        rolled = jnp.roll(blocks, -offset, axis=0)
        per_offset.append(lax.map(lambda pieces: block_stack(pieces[0], pieces[1]), (sources, rolled)))
    stacks = jnp.stack(per_offset, axis=1)
    return jnp.transpose(stacks, (0, 2, 1, 3)).reshape(N_CHAN * SRC, 2 * reach_steps, CB * LAGS)
```

```python
import functools

import jax
import jax.numpy as jnp
from jax import lax
from jax.experimental import pallas as pl
from jax.experimental.pallas import tpu as pltpu
from jax.sharding import PartitionSpec as P

SRC = 8
MAXLAG = 25
LAGS = 51
W2 = 64
EDGE = 128
HALF = 26
SLOT = 640
MEMBERS = 2
CHUNKS = ((0, 7), (7, 13))
MESH = pl.DeviceIdType.MESH


def split(value):
    high = value.astype(jnp.bfloat16)
    low = (value - high.astype(jnp.float32)).astype(jnp.bfloat16)
    return high, low


def correlate_kernel(
    sizes, x_hbm, out_ref,
    own, halo, normed, pieces, pieces_in, mine, sources_in, lagged, padded, partial,
    partial_in, sums, stacked,
    load_sem, halo_s, halo_r, piece_s, piece_r, src_s, src_r, part_s, part_r, sum_s, sum_r,
):
    n_chan, n_tm = sizes
    rows, length = own.shape
    members = MEMBERS
    groups = n_tm // members
    reach = 4
    offsets = [d for d in range(-reach, reach + 1) if d != 0]
    n_off = len(offsets)
    chan = lax.axis_index("chan")
    tm = lax.axis_index("tm")
    group = tm // members
    member = tm % members

    def chan_at(d):
        return lax.rem(chan + d + n_chan, n_chan)

    def tm_at(d):
        return lax.rem(tm + d + n_tm, n_tm)

    def mate(delta):
        return group * members + lax.rem(member + delta, members)

    def cousin(delta):
        return lax.rem(group + delta, groups) * members + member

    load = pltpu.make_async_copy(x_hbm, own, load_sem)
    load.start()

    barrier = pltpu.get_barrier_semaphore()

    def greet(c, t):
        pl.semaphore_signal(barrier, inc=1, device_id=(c, t), device_id_type=MESH)

    greet(chan, tm_at(1))
    greet(chan, tm_at(-1))
    for delta in range(1, members):
        greet(chan, mate(delta))
    for d in offsets:
        for delta in range(members):
            greet(chan_at(d), mate(delta))

    def greet_cousin(delta, carry):
        greet(chan, cousin(delta))
        return carry

    lax.fori_loop(1, groups, greet_cousin, 0)
    pl.semaphore_wait(barrier, 2 + members - 1 + n_off * members + groups - 1)

    def send(src, dst, s, r, c, t):
        return pltpu.make_async_remote_copy(
            src_ref=src, dst_ref=dst, send_sem=s, recv_sem=r,
            device_id=(c, t), device_id_type=MESH,
        )

    to_right = send(x_hbm.at[:, pl.ds(length - EDGE, EDGE)], halo.at[0], halo_s.at[0], halo_r.at[0], chan, tm_at(1))
    to_left = send(x_hbm.at[:, pl.ds(0, EDGE)], halo.at[1], halo_s.at[1], halo_r.at[1], chan, tm_at(-1))
    to_right.start()
    to_left.start()
    load.wait()

    row = lax.broadcasted_iota(jnp.int32, (512, 256), 0)
    col = lax.broadcasted_iota(jnp.int32, (512, 256), 1)
    band = (jnp.abs(row - EDGE - col) <= W2).astype(jnp.float32).astype(jnp.bfloat16)
    value = own[...]
    to_right.wait_recv()
    to_left.wait_recv()
    left = jnp.abs(halo[0]) * (tm > 0).astype(jnp.float32)
    right = jnp.abs(halo[1]) * (tm < n_tm - 1).astype(jnp.float32)
    magnitude = jnp.concatenate([left, jnp.abs(value), right], axis=1)
    high, low = split(magnitude)
    both = jnp.concatenate([high, low], axis=0)
    for part in range(length // 256):
        window = both[:, part * 256 : part * 256 + 512]
        total = jnp.dot(window, band, preferred_element_type=jnp.float32)
        level = (total[:rows] + total[rows:]) / (2 * W2 + 1) + 1e-05
        here = slice(part * 256, part * 256 + 256)
        normed[:, here] = (value[:, here] / level).astype(jnp.bfloat16).astype(jnp.float32)

    picked = jnp.concatenate([normed[pl.ds(q * (rows // SRC), 1), :] for q in range(SRC)], axis=0)
    mine[...] = jnp.concatenate([picked[:, :256], picked[:, 256:]], axis=0).astype(jnp.bfloat16)
    source_sends = []
    for o, d in enumerate(offsets):
        for delta in range(members):
            slot = (members - delta) % members
            source_sends.append(send(mine, sources_in.at[slot, o], src_s.at[slot, o], src_r.at[slot, o], chan_at(d), mate(delta)))
            source_sends[-1].start()

    for m in range(members):
        for pair in range(groups // 2):
            first = (2 * pair * members + m) * 8
            second = ((2 * pair + 1) * members + m) * 8
            block = jnp.concatenate([normed[pl.ds(first, 8), :], normed[pl.ds(second, 8), :]], axis=0)
            pieces[m, pl.ds(pair * 16, 16), :] = block.astype(jnp.bfloat16)
    piece_sends = []
    for delta in range(1, members):
        slot = members - delta
        target = lax.rem(member + delta, members)
        piece_sends.append(send(pieces.at[target], pieces_in.at[slot - 1], piece_s.at[slot - 1], piece_r.at[slot - 1], chan, mate(delta)))
        piece_sends[-1].start()

    count = rows // members
    blank = jnp.zeros((count, SLOT - length), jnp.float32)

    def place(slot, block):
        wide = jnp.concatenate([block.astype(jnp.float32), blank], axis=1)
        late = pltpu.roll(wide, HALF, 1)
        pair = jnp.concatenate([wide.reshape(groups, 8, SLOT), late.reshape(groups, 8, SLOT)], axis=1)
        lagged[:, pl.ds(slot * SLOT, SLOT)] = pair.reshape(groups * 16, SLOT).astype(jnp.bfloat16)

    place(0, pieces[member])
    for copy in piece_sends:
        copy.wait_recv()
    for slot in range(1, members):
        place(slot, pieces_in[slot - 1])
    for copy in source_sends:
        copy.wait_recv()
    n_src = n_off * SRC
    for slot in range(members):
        block = sources_in[slot].astype(jnp.float32)
        joined = jnp.concatenate([block[:, :SRC, :], block[:, SRC:, :]], axis=2).reshape(n_src, length)
        padded[:, pl.ds(slot * SLOT, SLOT)] = jnp.concatenate(
            [joined, jnp.zeros((n_src, SLOT - length), jnp.float32)], axis=1
        )

    scale = 1.0 / float(length * n_tm) ** 0.5

    def start_partials(chunk):
        first, last = CHUNKS[chunk]
        lanes = pl.ds(first * 128, (last - first) * 128)

        def one(delta, carry):
            to = lax.rem(group + delta, groups)
            send(
                partial.at[to, :, lanes], partial_in.at[delta - 1, :, lanes],
                part_s.at[chunk, delta - 1], part_r.at[chunk, delta - 1], chan, to * members + member,
            ).start()
            return carry

        lax.fori_loop(1, groups, one, 0)

    for chunk, (first, last) in enumerate(CHUNKS):
        for tile in range(first, last):
            wide = padded[...]
            shifted = jnp.concatenate(
                [pltpu.roll(wide, 2 * tile, 1) if tile else wide, pltpu.roll(wide, 2 * tile + 1, 1)], axis=0
            ).astype(jnp.bfloat16)
            product = lax.dot_general(
                lagged[...], shifted, (((1,), (1,)), ((), ())), preferred_element_type=jnp.float32
            )
            partial[:, :, tile * 128 : tile * 128 + 128] = (product * scale).astype(jnp.bfloat16).reshape(groups, 16, 128)
        start_partials(chunk)

    tall = 512
    k = lax.broadcasted_iota(jnp.int32, (tall, tall), 0)
    j = lax.broadcasted_iota(jnp.int32, (tall, tall), 1)
    b = jnp.bitwise_and(k, 7)
    late = jnp.bitwise_and(jnp.right_shift(k, 3), 1)
    tile = jnp.bitwise_and(jnp.right_shift(k, 4), 15)
    shift = 2 * tile + jnp.right_shift(k, 8)
    lag = shift - HALF * late + MAXLAG
    target = b * LAGS + lag
    fits = jnp.logical_and(jnp.logical_and(lag >= 0, tile < 13), target == j)
    order = fits.astype(jnp.float32).astype(jnp.bfloat16)

    def await_partials(delta, carry):
        for chunk, (first, last) in enumerate(CHUNKS):
            lanes = pl.ds(first * 128, (last - first) * 128)
            send(
                partial.at[0, :, lanes], partial_in.at[delta - 1, :, lanes],
                part_s.at[chunk, delta - 1], part_r.at[chunk, delta - 1], chan, cousin(delta),
            ).wait()
        return carry

    lax.fori_loop(1, groups, await_partials, 0)
    total = partial[group].astype(jnp.float32)
    for delta in range(1, groups):
        total = total + partial_in[delta - 1].astype(jnp.float32)
    tiles = [total[:, t * 128 : t * 128 + 128] for t in range(13)]
    tiles.append(jnp.zeros((48, 128), jnp.float32))
    turned = jnp.concatenate(tiles, axis=0).T
    flat = jnp.concatenate([turned[:n_src], turned[n_src:]], axis=1)
    high, low = split(flat)
    moved = jnp.dot(jnp.concatenate([high, low], axis=0), order, preferred_element_type=jnp.float32)
    sums[...] = moved[:n_src] + moved[n_src:]

    sum_sends = []
    for o, d in enumerate(offsets):
        part = pl.ds(o * SRC, SRC)
        sum_sends.append(send(sums.at[part, :], stacked.at[part, :], sum_s.at[o], sum_r.at[o], chan_at(-d), tm))
        sum_sends[-1].start()
    for copy in sum_sends:
        copy.wait_recv()
    out_ref[...] = stacked[...].reshape(n_off, SRC, 512)

    to_right.wait_send()
    to_left.wait_send()
    for copy in source_sends + piece_sends + sum_sends:
        copy.wait_send()


def body(sizes, strain_rate):
    rows, length = strain_rate.shape
    n_chan, n_tm = sizes
    members = MEMBERS
    groups = n_tm // members
    n_off = 8
    f32, bf16 = jnp.float32, jnp.bfloat16
    dma = pltpu.SemaphoreType.DMA
    stacks = pl.pallas_call(
        functools.partial(correlate_kernel, sizes),
        out_shape=jax.ShapeDtypeStruct((n_off, SRC, 512), f32),
        in_specs=[pl.BlockSpec(memory_space=pl.ANY)],
        out_specs=pl.BlockSpec(memory_space=pltpu.VMEM),
        scratch_shapes=[
            pltpu.VMEM((rows, length), f32),
            pltpu.VMEM((2, rows, EDGE), f32),
            pltpu.VMEM((rows, length), f32),
            pltpu.VMEM((members, rows // members, length), bf16),
            pltpu.VMEM((members - 1, rows // members, length), bf16),
            pltpu.VMEM((2 * SRC, length // 2), bf16),
            pltpu.VMEM((members, n_off, 2 * SRC, length // 2), bf16),
            pltpu.VMEM((groups * 16, members * SLOT), bf16),
            pltpu.VMEM((n_off * SRC, members * SLOT), f32),
            pltpu.VMEM((groups, 16, 13 * 128), bf16),
            pltpu.VMEM((groups - 1, 16, 13 * 128), bf16),
            pltpu.VMEM((n_off * SRC, 512), f32),
            pltpu.VMEM((n_off * SRC, 512), f32),
            dma, dma((2,)), dma((2,)), dma((members - 1,)), dma((members - 1,)),
            dma((members, n_off)), dma((members, n_off)),
            dma((len(CHUNKS), groups - 1)), dma((len(CHUNKS), groups - 1)),
            dma((n_off,)), dma((n_off,)),
        ],
        compiler_params=pltpu.CompilerParams(
            collective_id=0, has_side_effects=True, vmem_limit_bytes=48 * 1024 * 1024
        ),
    )(strain_rate)
    return jnp.transpose(stacks[:, :, : (rows // n_tm) * LAGS], (1, 0, 2))


def solution(mesh):
    sizes = (mesh.shape["chan"], mesh.shape["tm"])
    return jax.shard_map(
        functools.partial(body, sizes), mesh=mesh, in_specs=(P("chan", "tm"),),
        out_specs=P("chan", None, "tm"), check_vma=False,
    )
```

```python
import functools

import jax
import jax.numpy as jnp
from jax import lax
from jax.experimental import pallas as pl
from jax.experimental.pallas import tpu as pltpu
from jax.sharding import PartitionSpec as P

SRC = 8
MAXLAG = 25
LAGS = 51
W2 = 64
EDGE = 128
LATE = 26
SLOT = 640
REACH = 4
OFFSETS = [d for d in range(-REACH, REACH + 1) if d != 0]
TILES = 13
FAR_FIRST = (4, 3, 5, 2, 6, 1, 7)
CHUNKS = ((0, 4), (4, 8), (8, 13))
MESH = pl.DeviceIdType.MESH


def split(value):
    high = value.astype(jnp.bfloat16)
    low = (value - high.astype(jnp.float32)).astype(jnp.bfloat16)
    return high, low


def correlate_kernel(
    sizes, x_hbm, out_ref,
    own, edges, halo, normed, pieces, pieces_in, mine, sources_in, lagged, padded, partial,
    partial_in, sums, stacked,
    load_sem, ready, halo_s, halo_r, piece_s, piece_r, src_s, src_r, part_s, part_r, sum_s, sum_r,
):
    n_chan, n_tm = sizes
    rows, length = own.shape
    groups = n_tm // 4
    chan = lax.axis_index("chan")
    tm = lax.axis_index("tm")
    group, pair, core = tm // 4, (tm // 2) % 2, tm % 2

    def chan_at(d):
        return lax.rem(chan + d + n_chan, n_chan)

    def tm_at(d):
        return lax.rem(tm + d + n_tm, n_tm)

    def mate(across, other):
        return group * 4 + lax.rem(pair + across, 2) * 2 + lax.rem(core + other, 2)

    def cousin(delta):
        return lax.rem(group + delta, groups) * 4 + pair * 2 + core

    mates = ((0, 1), (1, 0), (1, 1))

    load = pltpu.make_async_copy(x_hbm, own, load_sem)
    load.start()

    barrier = pltpu.get_barrier_semaphore()

    def greet(c, t):
        pl.semaphore_signal(barrier, inc=1, device_id=(c, t), device_id_type=MESH)

    greet(chan, tm_at(1))
    greet(chan, tm_at(-1))
    for d in OFFSETS:
        greet(chan_at(d), tm)
    for across, other in mates:
        greet(chan, mate(across, other))
    for delta in range(1, groups):
        greet(chan, cousin(delta))

    load.wait()
    value = own[...]
    half = rows // 2
    lane = lax.broadcasted_iota(jnp.int32, (half, EDGE), 1)
    first_edge = jnp.abs(value[:, :EDGE])
    last_edge = jnp.abs(value[:, length - EDGE :])
    edges[0] = jnp.where(lane < W2, pltpu.roll(last_edge[:half], W2, 1), last_edge[half:]).astype(jnp.bfloat16)
    edges[1] = jnp.where(lane < W2, first_edge[:half], pltpu.roll(first_edge[half:], W2, 1)).astype(jnp.bfloat16)
    row = lax.broadcasted_iota(jnp.int32, (512, 256), 0)
    col = lax.broadcasted_iota(jnp.int32, (512, 256), 1)
    band = (jnp.abs(row - EDGE - col) <= W2).astype(jnp.float32).astype(jnp.bfloat16)

    pl.semaphore_wait(barrier, 2 + len(OFFSETS) + len(mates) + groups - 1)

    def send(src, dst, s, r, c, t):
        return pltpu.make_async_remote_copy(
            src_ref=src, dst_ref=dst, send_sem=s, recv_sem=r,
            device_id=(c, t), device_id_type=MESH,
        )

    to_right = send(edges.at[0], halo.at[0], halo_s.at[0], halo_r.at[0], chan, tm_at(1))
    to_left = send(edges.at[1], halo.at[1], halo_s.at[1], halo_r.at[1], chan, tm_at(-1))
    to_right.start()
    to_left.start()
    for across, other in mates:
        pl.semaphore_signal(ready, inc=1, device_id=(chan, mate(across, other)), device_id_type=MESH)

    to_right.wait_recv()
    to_left.wait_recv()
    before = halo[0].astype(jnp.float32) * (tm > 0).astype(jnp.float32)
    after = halo[1].astype(jnp.float32) * (tm < n_tm - 1).astype(jnp.float32)
    left = jnp.concatenate([pltpu.roll(before, W2, 1), before], axis=0)
    right = jnp.concatenate([after, pltpu.roll(after, W2, 1)], axis=0)
    magnitude = jnp.concatenate([left, jnp.abs(value), right], axis=1)
    high, low = split(magnitude)
    both = jnp.concatenate([high, low], axis=0)
    for part in range(length // 256):
        window = both[:, part * 256 : part * 256 + 512]
        total = jnp.dot(window, band, preferred_element_type=jnp.float32)
        level = (total[:rows] + total[rows:]) / (2 * W2 + 1) + 1e-05
        here = slice(part * 256, part * 256 + 256)
        normed[:, here] = (value[:, here] / level).astype(jnp.bfloat16).astype(jnp.float32)

    picked = jnp.concatenate([normed[pl.ds(q * (rows // SRC), 1), :] for q in range(SRC)], axis=0)
    mine[...] = jnp.concatenate([picked[:, :256], picked[:, 256:]], axis=0).astype(jnp.bfloat16)
    source_sends = []
    pl.semaphore_wait(ready, len(mates))
    for across in range(2):
        for o, d in enumerate(OFFSETS):
            side, place_o = o // REACH, o % REACH
            slot = across * 2 + lax.rem(core + side, 2)
            to = group * 4 + lax.rem(pair + across, 2) * 2 + side
            source_sends.append(
                send(mine, sources_in.at[slot, place_o], src_s.at[across, o], src_r.at[slot, place_o], chan_at(d), to)
            )
            source_sends[-1].start()

    for p in range(2):
        for g in range(groups):
            pieces[p, pl.ds(g * 16, 16), :] = normed[pl.ds(g * 32 + p * 16, 16), :].astype(jnp.bfloat16)
    def piece_send(src, slot, across, other):
        return send(src, pieces_in.at[slot], piece_s.at[slot], piece_r.at[slot], chan, mate(across, other))

    piece_sends = [
        piece_send(pieces.at[pair], 0, 0, 1),
        piece_send(pieces.at[1 - pair], 1, 1, 0),
        piece_send(pieces_in.at[1], 2, 0, 1),
    ]
    piece_sends[1].start()
    piece_sends[0].start()

    count = groups * 16
    blank = jnp.zeros((count, SLOT - length), jnp.float32)

    def place(slot, block):
        wide = jnp.concatenate([block.astype(jnp.float32), blank], axis=1)
        late = pltpu.roll(wide, LATE, 1)
        two = jnp.concatenate([wide.reshape(groups, 16, SLOT), late.reshape(groups, 16, SLOT)], axis=1)
        lagged[:, slot * SLOT : slot * SLOT + SLOT] = two.reshape(groups * 32, SLOT).astype(jnp.bfloat16)

    place(0, pieces[pair])
    piece_sends[0].wait_recv()
    place(1, pieces_in[0])
    piece_sends[1].wait_recv()
    piece_sends[2].start()
    place(2, pieces_in[1])
    piece_sends[2].wait_recv()
    place(3, pieces_in[2])
    n_src = REACH * SRC
    for slot in range(4):
        for place_o in range(REACH):
            send(mine, sources_in.at[slot, place_o], src_s.at[0, 0], src_r.at[slot, place_o], chan_at(1), tm).wait_recv()
        block = sources_in[slot].astype(jnp.float32)
        joined = jnp.concatenate([block[:, :SRC, :], block[:, SRC:, :]], axis=2).reshape(n_src, length)
        padded[:, slot * SLOT : slot * SLOT + SLOT] = jnp.concatenate(
            [joined, jnp.zeros((n_src, SLOT - length), jnp.float32)], axis=1
        )

    scale = 1.0 / float(length * n_tm) ** 0.5

    def partial_copy(chunk, delta):
        first, last = CHUNKS[chunk]
        to = lax.rem(group + delta, groups)
        part = pl.ds(first, last - first)
        return send(
            partial.at[to, part], partial_in.at[delta - 1, part],
            part_s.at[chunk, delta - 1], part_r.at[chunk, delta - 1], chan, cousin(delta),
        )

    def product(shifts):
        wide = padded[...]
        shifted = jnp.concatenate([pltpu.roll(wide, c, 1) if c else wide for c in shifts], axis=0)
        result = lax.dot_general(
            lagged[...], shifted.astype(jnp.bfloat16), (((1,), (1,)), ((), ())),
            preferred_element_type=jnp.float32,
        )
        return (result * scale).reshape(groups, 2, 16, len(shifts) * n_src)

    for step in range(4):
        if step < 3:
            result = product(range(8 * step, 8 * step + 8)).astype(jnp.bfloat16)
            for late in range(2):
                for side in range(2):
                    partial[:, 4 * step + 2 * late + side] = result[:, late, :, side * 128 : side * 128 + 128]
        else:
            result = product(range(24, 26))
            partial[:, 12] = jnp.concatenate([result[:, 0], result[:, 1]], axis=2).astype(jnp.bfloat16)
        for chunk, (first, last) in enumerate(CHUNKS):
            if last == min(4 * step + 4, TILES):
                for delta in FAR_FIRST:
                    partial_copy(chunk, delta).start()

    tall = 512
    k = lax.broadcasted_iota(jnp.int32, (tall, tall), 0)
    j = lax.broadcasted_iota(jnp.int32, (tall, tall), 1)
    b = jnp.bitwise_and(k, 7)
    tile = jnp.bitwise_and(jnp.right_shift(k, 3), 15)
    quarter = jnp.right_shift(k, 7)
    mixed = tile == 12
    late = jnp.where(mixed, jnp.right_shift(quarter, 1), jnp.bitwise_and(jnp.right_shift(tile, 1), 1))
    shift = jnp.where(
        mixed, 24 + jnp.bitwise_and(quarter, 1),
        8 * jnp.right_shift(tile, 2) + 4 * jnp.bitwise_and(tile, 1) + quarter,
    )
    lag = shift - LATE * late + MAXLAG
    fits = jnp.logical_and(jnp.logical_and(lag >= 0, tile < TILES), b * LAGS + lag == j)
    order = fits.astype(jnp.float32).astype(jnp.bfloat16)

    for chunk in range(len(CHUNKS)):
        for delta in range(1, groups):
            partial_copy(chunk, delta).wait_recv()
    total = partial[group].astype(jnp.float32)
    for delta in range(1, groups):
        total = total + partial_in[delta - 1].astype(jnp.float32)
    spare = jnp.zeros((24, 128), jnp.float32)
    stack = []
    for owner in range(2):
        stack += [total[:, owner * 8 : owner * 8 + 8, :].reshape(TILES * 8, 128), spare]
    turned = jnp.concatenate(stack, axis=0).T
    flat = jnp.concatenate(
        [
            jnp.concatenate(
                [turned[n_src * s : n_src * s + n_src, owner * 128 : owner * 128 + 128] for s in range(4)], axis=1
            )
            for owner in range(2)
        ],
        axis=0,
    )
    high, low = split(flat)
    moved = jnp.dot(jnp.concatenate([high, low], axis=0), order, preferred_element_type=jnp.float32)
    sums[...] = moved[: 2 * n_src] + moved[2 * n_src :]

    sum_sends = []
    for place_o in range(REACH):
        low_d, high_d = OFFSETS[place_o], OFFSETS[REACH + place_o]
        back = chan_at(-low_d - core * (high_d - low_d))
        for owner in range(2):
            o = core * REACH + place_o
            sum_sends.append(
                send(
                    sums.at[pl.ds((owner * REACH + place_o) * SRC, SRC), :], stacked.at[o],
                    sum_s.at[owner, place_o], sum_r.at[o], back, group * 4 + pair * 2 + owner,
                )
            )
            sum_sends[-1].start()
    for o in range(2 * REACH):
        send(sums.at[pl.ds(0, SRC), :], stacked.at[o], sum_s.at[0, 0], sum_r.at[o], chan_at(1), tm).wait_recv()
    out_ref[...] = stacked[...]

    to_right.wait_send()
    to_left.wait_send()
    for copy in source_sends + piece_sends + sum_sends:
        copy.wait_send()
    for chunk in range(len(CHUNKS)):
        for delta in range(1, groups):
            partial_copy(chunk, delta).wait_send()


def body(sizes, strain_rate):
    rows, length = strain_rate.shape
    n_chan, n_tm = sizes
    groups = n_tm // 4
    n_off = len(OFFSETS)
    f32, bf16 = jnp.float32, jnp.bfloat16
    dma = pltpu.SemaphoreType.DMA
    stacks = pl.pallas_call(
        functools.partial(correlate_kernel, sizes),
        out_shape=jax.ShapeDtypeStruct((n_off, SRC, 512), f32),
        in_specs=[pl.BlockSpec(memory_space=pl.ANY)],
        out_specs=pl.BlockSpec(memory_space=pltpu.VMEM),
        scratch_shapes=[
            pltpu.VMEM((rows, length), f32),
            pltpu.VMEM((2, rows // 2, EDGE), bf16),
            pltpu.VMEM((2, rows // 2, EDGE), bf16),
            pltpu.VMEM((rows, length), f32),
            pltpu.VMEM((2, rows // 2, length), bf16),
            pltpu.VMEM((3, rows // 2, length), bf16),
            pltpu.VMEM((2 * SRC, length // 2), bf16),
            pltpu.VMEM((4, REACH, 2 * SRC, length // 2), bf16),
            pltpu.VMEM((groups * 32, 4 * SLOT), bf16),
            pltpu.VMEM((REACH * SRC, 4 * SLOT), f32),
            pltpu.VMEM((groups, TILES, 16, 128), bf16),
            pltpu.VMEM((groups - 1, TILES, 16, 128), bf16),
            pltpu.VMEM((2 * REACH * SRC, 512), f32),
            pltpu.VMEM((n_off, SRC, 512), f32),
            dma, pltpu.SemaphoreType.REGULAR, dma((2,)), dma((2,)), dma((3,)), dma((3,)),
            dma((2, n_off)), dma((4, REACH)),
            dma((len(CHUNKS), groups - 1)), dma((len(CHUNKS), groups - 1)),
            dma((2, REACH)), dma((n_off,)),
        ],
        compiler_params=pltpu.CompilerParams(
            collective_id=0, has_side_effects=True, vmem_limit_bytes=48 * 1024 * 1024
        ),
    )(strain_rate)
    return jnp.transpose(stacks[:, :, : (rows // n_tm) * LAGS], (1, 0, 2))


def solution(mesh):
    sizes = (mesh.shape["chan"], mesh.shape["tm"])
    return jax.shard_map(
        functools.partial(body, sizes), mesh=mesh, in_specs=(P("chan", "tm"),),
        out_specs=P("chan", None, "tm"), check_vma=False,
    )
```

```python
import functools

import jax
import jax.numpy as jnp
from jax import lax
from jax.experimental import pallas as pl
from jax.experimental.pallas import tpu as pltpu
from jax.sharding import PartitionSpec as P

SRC = 8
MAXLAG = 25
LAGS = 51
W2 = 64
EDGE = 128
LATE = 26
SLOT = 640
REACH = 4
OFFSETS = (-4, 3, -2, 1, 4, -3, 2, -1)
PLACES = tuple(d + REACH if d < 0 else d + REACH - 1 for d in OFFSETS)
TILES = 13
FAR_FIRST = (4, 3, 5, 2, 6, 1, 7)
CHUNKS = ((0, 4), (4, 8), (8, 13))
MESH = pl.DeviceIdType.MESH


def split(value):
    high = value.astype(jnp.bfloat16)
    low = (value - high.astype(jnp.float32)).astype(jnp.bfloat16)
    return high, low


def correlate_kernel(
    sizes, x_hbm, out_ref,
    own, edges, halo, normed, pieces, pieces_in, mine, sources_in, lagged, padded, partial,
    partial_in, sums, stacked,
    load_sem, ready, halo_s, halo_r, piece_s, piece_r, src_s, src_r, part_s, part_r, sum_s, sum_r,
):
    n_chan, n_tm = sizes
    rows, length = own.shape
    groups = n_tm // 4
    chan = lax.axis_index("chan")
    tm = lax.axis_index("tm")
    group, pair, core = tm // 4, (tm // 2) % 2, tm % 2

    def chan_at(d):
        return lax.rem(chan + d + n_chan, n_chan)

    def tm_at(d):
        return lax.rem(tm + d + n_tm, n_tm)

    def mate(across, other):
        return group * 4 + lax.rem(pair + across, 2) * 2 + lax.rem(core + other, 2)

    def cousin(delta):
        return lax.rem(group + delta, groups) * 4 + pair * 2 + core

    mates = ((0, 1), (1, 0), (1, 1))

    load = pltpu.make_async_copy(x_hbm, own, load_sem)
    load.start()

    barrier = pltpu.get_barrier_semaphore()

    def greet(c, t):
        pl.semaphore_signal(barrier, inc=1, device_id=(c, t), device_id_type=MESH)

    greet(chan, tm_at(1))
    greet(chan, tm_at(-1))
    for d in OFFSETS:
        greet(chan_at(d), tm)
    for across, other in mates:
        greet(chan, mate(across, other))
    for delta in range(1, groups):
        greet(chan, cousin(delta))

    load.wait()
    value = own[...]
    half = rows // 2
    lane = lax.broadcasted_iota(jnp.int32, (half, EDGE), 1)
    first_edge = jnp.abs(value[:, :EDGE])
    last_edge = jnp.abs(value[:, length - EDGE :])
    edges[0] = jnp.where(lane < W2, pltpu.roll(last_edge[:half], W2, 1), last_edge[half:]).astype(jnp.bfloat16)
    edges[1] = jnp.where(lane < W2, first_edge[:half], pltpu.roll(first_edge[half:], W2, 1)).astype(jnp.bfloat16)
    row = lax.broadcasted_iota(jnp.int32, (512, 256), 0)
    col = lax.broadcasted_iota(jnp.int32, (512, 256), 1)
    band = (jnp.abs(row - EDGE - col) <= W2).astype(jnp.float32).astype(jnp.bfloat16)

    pl.semaphore_wait(barrier, 2 + len(OFFSETS) + len(mates) + groups - 1)

    def send(src, dst, s, r, c, t):
        return pltpu.make_async_remote_copy(
            src_ref=src, dst_ref=dst, send_sem=s, recv_sem=r,
            device_id=(c, t), device_id_type=MESH,
        )

    to_right = send(edges.at[0], halo.at[0], halo_s.at[0], halo_r.at[0], chan, tm_at(1))
    to_left = send(edges.at[1], halo.at[1], halo_s.at[1], halo_r.at[1], chan, tm_at(-1))
    to_right.start()
    to_left.start()
    for across, other in mates:
        pl.semaphore_signal(ready, inc=1, device_id=(chan, mate(across, other)), device_id_type=MESH)

    to_right.wait_recv()
    to_left.wait_recv()
    before = halo[0].astype(jnp.float32) * (tm > 0).astype(jnp.float32)
    after = halo[1].astype(jnp.float32) * (tm < n_tm - 1).astype(jnp.float32)
    left = jnp.concatenate([pltpu.roll(before, W2, 1), before], axis=0)
    right = jnp.concatenate([after, pltpu.roll(after, W2, 1)], axis=0)
    magnitude = jnp.concatenate([left, jnp.abs(value), right], axis=1)
    high, low = split(magnitude)
    both = jnp.concatenate([high, low], axis=0)
    for part in range(length // 256):
        window = both[:, part * 256 : part * 256 + 512]
        total = jnp.dot(window, band, preferred_element_type=jnp.float32)
        level = (total[:rows] + total[rows:]) / (2 * W2 + 1) + 1e-05
        here = slice(part * 256, part * 256 + 256)
        normed[:, here] = (value[:, here] / level).astype(jnp.bfloat16).astype(jnp.float32)

    picked = jnp.concatenate([normed[pl.ds(q * (rows // SRC), 1), :] for q in range(SRC)], axis=0)
    mine[...] = jnp.concatenate([picked[:, :256], picked[:, 256:]], axis=0).astype(jnp.bfloat16)
    source_sends = []
    pl.semaphore_wait(ready, len(mates))
    for across in range(2):
        for o, d in enumerate(OFFSETS):
            side, place_o = o // REACH, o % REACH
            slot = across * 2 + lax.rem(core + side, 2)
            to = group * 4 + lax.rem(pair + across, 2) * 2 + side
            source_sends.append(
                send(mine, sources_in.at[slot, place_o], src_s.at[across, o], src_r.at[slot, place_o], chan_at(d), to)
            )
            source_sends[-1].start()

    for p in range(2):
        for g in range(groups):
            pieces[p, pl.ds(g * 16, 16), :] = normed[pl.ds(g * 32 + p * 16, 16), :].astype(jnp.bfloat16)
    def piece_send(src, slot, across, other):
        return send(src, pieces_in.at[slot], piece_s.at[slot], piece_r.at[slot], chan, mate(across, other))

    piece_sends = [
        piece_send(pieces.at[pair], 0, 0, 1),
        piece_send(pieces.at[1 - pair], 1, 1, 0),
        piece_send(pieces_in.at[1], 2, 0, 1),
    ]
    piece_sends[1].start()
    piece_sends[0].start()

    count = groups * 16
    blank = jnp.zeros((count, SLOT - length), jnp.float32)

    def place(slot, block):
        wide = jnp.concatenate([block.astype(jnp.float32), blank], axis=1)
        late = pltpu.roll(wide, LATE, 1)
        two = jnp.concatenate([wide.reshape(groups, 16, SLOT), late.reshape(groups, 16, SLOT)], axis=1)
        lagged[:, slot * SLOT : slot * SLOT + SLOT] = two.reshape(groups * 32, SLOT).astype(jnp.bfloat16)

    place(0, pieces[pair])
    piece_sends[0].wait_recv()
    place(1, pieces_in[0])
    piece_sends[1].wait_recv()
    piece_sends[2].start()
    place(2, pieces_in[1])
    piece_sends[2].wait_recv()
    place(3, pieces_in[2])
    n_src = REACH * SRC
    for slot in range(4):
        for place_o in range(REACH):
            send(mine, sources_in.at[slot, place_o], src_s.at[0, 0], src_r.at[slot, place_o], chan_at(1), tm).wait_recv()
        block = sources_in[slot].astype(jnp.float32)
        joined = jnp.concatenate([block[:, :SRC, :], block[:, SRC:, :]], axis=2).reshape(n_src, length)
        padded[:, slot * SLOT : slot * SLOT + SLOT] = jnp.concatenate(
            [joined, jnp.zeros((n_src, SLOT - length), jnp.float32)], axis=1
        )

    scale = 1.0 / float(length * n_tm) ** 0.5

    def partial_copy(chunk, delta):
        first, last = CHUNKS[chunk]
        to = lax.rem(group + delta, groups)
        part = pl.ds(first, last - first)
        return send(
            partial.at[to, part], partial_in.at[delta - 1, part],
            part_s.at[chunk, delta - 1], part_r.at[chunk, delta - 1], chan, cousin(delta),
        )

    def product(shifts):
        wide = padded[...]
        shifted = jnp.concatenate([pltpu.roll(wide, c, 1) if c else wide for c in shifts], axis=0)
        result = lax.dot_general(
            lagged[...], shifted.astype(jnp.bfloat16), (((1,), (1,)), ((), ())),
            preferred_element_type=jnp.float32,
        )
        return (result * scale).reshape(groups, 2, 16, len(shifts) * n_src)

    for step in range(4):
        if step < 3:
            result = product(range(8 * step, 8 * step + 8)).astype(jnp.bfloat16)
            for late in range(2):
                for side in range(2):
                    partial[:, 4 * step + 2 * late + side] = result[:, late, :, side * 128 : side * 128 + 128]
        else:
            result = product(range(24, 26))
            partial[:, 12] = jnp.concatenate([result[:, 0], result[:, 1]], axis=2).astype(jnp.bfloat16)
        for chunk, (first, last) in enumerate(CHUNKS):
            if last == min(4 * step + 4, TILES):
                for delta in FAR_FIRST:
                    partial_copy(chunk, delta).start()

    tall = 512
    k = lax.broadcasted_iota(jnp.int32, (tall, tall), 0)
    j = lax.broadcasted_iota(jnp.int32, (tall, tall), 1)
    b = jnp.bitwise_and(k, 7)
    tile = jnp.bitwise_and(jnp.right_shift(k, 3), 15)
    quarter = jnp.right_shift(k, 7)
    mixed = tile == 12
    late = jnp.where(mixed, jnp.right_shift(quarter, 1), jnp.bitwise_and(jnp.right_shift(tile, 1), 1))
    shift = jnp.where(
        mixed, 24 + jnp.bitwise_and(quarter, 1),
        8 * jnp.right_shift(tile, 2) + 4 * jnp.bitwise_and(tile, 1) + quarter,
    )
    lag = shift - LATE * late + MAXLAG
    fits = jnp.logical_and(jnp.logical_and(lag >= 0, tile < TILES), b * LAGS + lag == j)
    order = fits.astype(jnp.float32).astype(jnp.bfloat16)

    for chunk in range(len(CHUNKS)):
        for delta in range(1, groups):
            partial_copy(chunk, delta).wait_recv()
    total = partial[group].astype(jnp.float32)
    for delta in range(1, groups):
        total = total + partial_in[delta - 1].astype(jnp.float32)
    spare = jnp.zeros((24, 128), jnp.float32)
    stack = []
    for owner in range(2):
        stack += [total[:, owner * 8 : owner * 8 + 8, :].reshape(TILES * 8, 128), spare]
    turned = jnp.concatenate(stack, axis=0).T
    flat = jnp.concatenate(
        [
            jnp.concatenate(
                [turned[n_src * s : n_src * s + n_src, owner * 128 : owner * 128 + 128] for s in range(4)], axis=1
            )
            for owner in range(2)
        ],
        axis=0,
    )
    high, low = split(flat)
    moved = jnp.dot(jnp.concatenate([high, low], axis=0), order, preferred_element_type=jnp.float32)
    sums[...] = moved[: 2 * n_src] + moved[2 * n_src :]

    sum_sends = []
    for place_o in range(REACH):
        low_d, high_d = OFFSETS[place_o], OFFSETS[REACH + place_o]
        back = chan_at(-low_d - core * (high_d - low_d))
        for owner in range(2):
            o = PLACES[place_o] + core * (PLACES[REACH + place_o] - PLACES[place_o])
            sum_sends.append(
                send(
                    sums.at[pl.ds((owner * REACH + place_o) * SRC, SRC), :], stacked.at[o],
                    sum_s.at[owner, place_o], sum_r.at[o], back, group * 4 + pair * 2 + owner,
                )
            )
            sum_sends[-1].start()
    for o in range(2 * REACH):
        send(sums.at[pl.ds(0, SRC), :], stacked.at[o], sum_s.at[0, 0], sum_r.at[o], chan_at(1), tm).wait_recv()
    out_ref[...] = stacked[...]

    to_right.wait_send()
    to_left.wait_send()
    for copy in source_sends + piece_sends + sum_sends:
        copy.wait_send()
    for chunk in range(len(CHUNKS)):
        for delta in range(1, groups):
            partial_copy(chunk, delta).wait_send()


def body(sizes, strain_rate):
    rows, length = strain_rate.shape
    n_chan, n_tm = sizes
    groups = n_tm // 4
    n_off = len(OFFSETS)
    f32, bf16 = jnp.float32, jnp.bfloat16
    dma = pltpu.SemaphoreType.DMA
    stacks = pl.pallas_call(
        functools.partial(correlate_kernel, sizes),
        out_shape=jax.ShapeDtypeStruct((n_off, SRC, 512), f32),
        in_specs=[pl.BlockSpec(memory_space=pl.ANY)],
        out_specs=pl.BlockSpec(memory_space=pltpu.VMEM),
        scratch_shapes=[
            pltpu.VMEM((rows, length), f32),
            pltpu.VMEM((2, rows // 2, EDGE), bf16),
            pltpu.VMEM((2, rows // 2, EDGE), bf16),
            pltpu.VMEM((rows, length), f32),
            pltpu.VMEM((2, rows // 2, length), bf16),
            pltpu.VMEM((3, rows // 2, length), bf16),
            pltpu.VMEM((2 * SRC, length // 2), bf16),
            pltpu.VMEM((4, REACH, 2 * SRC, length // 2), bf16),
            pltpu.VMEM((groups * 32, 4 * SLOT), bf16),
            pltpu.VMEM((REACH * SRC, 4 * SLOT), f32),
            pltpu.VMEM((groups, TILES, 16, 128), bf16),
            pltpu.VMEM((groups - 1, TILES, 16, 128), bf16),
            pltpu.VMEM((2 * REACH * SRC, 512), f32),
            pltpu.VMEM((n_off, SRC, 512), f32),
            dma, pltpu.SemaphoreType.REGULAR, dma((2,)), dma((2,)), dma((3,)), dma((3,)),
            dma((2, n_off)), dma((4, REACH)),
            dma((len(CHUNKS), groups - 1)), dma((len(CHUNKS), groups - 1)),
            dma((2, REACH)), dma((n_off,)),
        ],
        compiler_params=pltpu.CompilerParams(
            collective_id=0, has_side_effects=True, vmem_limit_bytes=55000 * 1024
        ),
    )(strain_rate)
    return jnp.transpose(stacks[:, :, : (rows // n_tm) * LAGS], (1, 0, 2))


def solution(mesh):
    sizes = (mesh.shape["chan"], mesh.shape["tm"])
    return jax.shard_map(
        functools.partial(body, sizes), mesh=mesh, in_specs=(P("chan", "tm"),),
        out_specs=P("chan", None, "tm"), check_vma=False,
    )
```

```python
import functools

import jax
import jax.numpy as jnp
from jax import lax
from jax.experimental import pallas as pl
from jax.experimental.pallas import tpu as pltpu
from jax.sharding import PartitionSpec as P

SRC = 8
MAXLAG = 25
LAGS = 51
W2 = 64
EDGE = 128
LATE = 26
SLOT = 640
REACH = 4
OFFSETS = (-4, 3, -2, 1, 4, -3, 2, -1)
PLACES = tuple(d + REACH if d < 0 else d + REACH - 1 for d in OFFSETS)
TILES = 13
FAR_FIRST = (4, 3, 5, 2, 6, 1, 7)
CHUNKS = ((0, 4), (4, 8), (8, 13))
MESH = pl.DeviceIdType.MESH


def split(value):
    high = value.astype(jnp.bfloat16)
    low = (value - high.astype(jnp.float32)).astype(jnp.bfloat16)
    return high, low


def correlate_kernel(
    sizes, x_hbm, out_ref,
    own, edges, halo, normed, pieces, pieces_in, mine, sources_in, lagged, padded, partial,
    partial_in, sums, stacked,
    load_sem, ready, halo_s, halo_r, piece_s, piece_r, src_s, src_r, part_s, part_r, sum_s, sum_r,
):
    n_chan, n_tm = sizes
    rows, length = own.shape
    groups = n_tm // 4
    chan = lax.axis_index("chan")
    tm = lax.axis_index("tm")
    group, pair, core = tm // 4, (tm // 2) % 2, tm % 2

    def chan_at(d):
        return lax.rem(chan + d + n_chan, n_chan)

    def tm_at(d):
        return lax.rem(tm + d + n_tm, n_tm)

    def mate(across, other):
        return group * 4 + lax.rem(pair + across, 2) * 2 + lax.rem(core + other, 2)

    def cousin(delta):
        return lax.rem(group + delta, groups) * 4 + pair * 2 + core

    mates = ((0, 1), (1, 0), (1, 1))

    load = pltpu.make_async_copy(x_hbm, own, load_sem)
    load.start()

    barrier = pltpu.get_barrier_semaphore()

    def greet(c, t):
        pl.semaphore_signal(barrier, inc=1, device_id=(c, t), device_id_type=MESH)

    greet(chan, tm_at(1))
    greet(chan, tm_at(-1))
    for d in OFFSETS:
        greet(chan_at(d), tm)
    for across, other in mates:
        greet(chan, mate(across, other))
    for delta in range(1, groups):
        greet(chan, cousin(delta))

    load.wait()
    value = own[...]
    half = rows // 2
    lane = lax.broadcasted_iota(jnp.int32, (half, EDGE), 1)
    first_edge = jnp.abs(value[:, :EDGE])
    last_edge = jnp.abs(value[:, length - EDGE :])
    edges[0] = jnp.where(lane < W2, pltpu.roll(last_edge[:half], W2, 1), last_edge[half:]).astype(jnp.bfloat16)
    edges[1] = jnp.where(lane < W2, first_edge[:half], pltpu.roll(first_edge[half:], W2, 1)).astype(jnp.bfloat16)
    row = lax.broadcasted_iota(jnp.int32, (512, 256), 0)
    col = lax.broadcasted_iota(jnp.int32, (512, 256), 1)
    band = (jnp.abs(row - EDGE - col) <= W2).astype(jnp.float32).astype(jnp.bfloat16)

    pl.semaphore_wait(barrier, 2 + len(OFFSETS) + len(mates) + groups - 1)

    def send(src, dst, s, r, c, t):
        return pltpu.make_async_remote_copy(
            src_ref=src, dst_ref=dst, send_sem=s, recv_sem=r,
            device_id=(c, t), device_id_type=MESH,
        )

    to_right = send(edges.at[0], halo.at[0], halo_s.at[0], halo_r.at[0], chan, tm_at(1))
    to_left = send(edges.at[1], halo.at[1], halo_s.at[1], halo_r.at[1], chan, tm_at(-1))
    to_right.start()
    to_left.start()
    for across, other in mates:
        pl.semaphore_signal(ready, inc=1, device_id=(chan, mate(across, other)), device_id_type=MESH)

    def normalise(window, here):
        high, low = split(window)
        total = jnp.dot(
            jnp.concatenate([high, low], axis=0), band[: window.shape[1], : here.stop - here.start],
            preferred_element_type=jnp.float32,
        )
        level = (total[:rows] + total[rows:]) / (2 * W2 + 1) + 1e-05
        normed[:, here] = (value[:, here] / level).astype(jnp.bfloat16).astype(jnp.float32)

    def piece_send(src, kind, slot, across, other):
        n = 2 * slot + kind
        return send(src, pieces_in.at[kind, slot], piece_s.at[n], piece_r.at[n], chan, mate(across, other))

    beside = [piece_send(pieces.at[kind, pair], kind, 0, 0, 1) for kind in range(2)]
    between = [piece_send(pieces.at[kind, 1 - pair], kind, 1, 1, 0) for kind in range(2)]
    onward = [piece_send(pieces_in.at[kind, 1], kind, 2, 0, 1) for kind in range(2)]

    def give_pieces(kind):
        for p in range(2):
            for g in range(groups):
                at = pl.ds(g * 32 + p * 16, 16)
                if kind == 0:
                    block = normed[at, EDGE : length - EDGE]
                else:
                    block = jnp.concatenate([normed[at, :EDGE], normed[at, length - EDGE :]], axis=1)
                pieces[kind, p, pl.ds(g * 16, 16), :] = block.astype(jnp.bfloat16)
        between[kind].start()
        beside[kind].start()

    absolute = jnp.abs(value)
    normalise(absolute, slice(EDGE, length - EDGE))
    give_pieces(0)

    to_right.wait_recv()
    to_left.wait_recv()
    before = halo[0].astype(jnp.float32) * (tm > 0).astype(jnp.float32)
    after = halo[1].astype(jnp.float32) * (tm < n_tm - 1).astype(jnp.float32)
    left = jnp.concatenate([pltpu.roll(before, W2, 1), before], axis=0)
    right = jnp.concatenate([after, pltpu.roll(after, W2, 1)], axis=0)
    normalise(jnp.concatenate([left, absolute[:, : 2 * EDGE]], axis=1), slice(0, EDGE))
    normalise(jnp.concatenate([absolute[:, length - 2 * EDGE :], right], axis=1), slice(length - EDGE, length))

    picked = jnp.concatenate([normed[pl.ds(q * (rows // SRC), 1), :] for q in range(SRC)], axis=0)
    mine[...] = jnp.concatenate([picked[:, :256], picked[:, 256:]], axis=0).astype(jnp.bfloat16)
    source_sends = []
    pl.semaphore_wait(ready, len(mates))
    for across in range(2):
        for o, d in enumerate(OFFSETS):
            side, place_o = o // REACH, o % REACH
            slot = across * 2 + lax.rem(core + side, 2)
            to = group * 4 + lax.rem(pair + across, 2) * 2 + side
            source_sends.append(
                send(mine, sources_in.at[slot, place_o], src_s.at[across, o], src_r.at[slot, place_o], chan_at(d), to)
            )
            source_sends[-1].start()

    give_pieces(1)

    count = groups * 16
    blank = jnp.zeros((count, SLOT - length), jnp.float32)

    def place(slot, middle, ends):
        middle, ends = middle.astype(jnp.float32), ends.astype(jnp.float32)
        wide = jnp.concatenate([ends[:, :EDGE], middle, ends[:, EDGE:], blank], axis=1)
        late = pltpu.roll(wide, LATE, 1)
        two = jnp.concatenate([wide.reshape(groups, 16, SLOT), late.reshape(groups, 16, SLOT)], axis=1)
        lagged[:, slot * SLOT : slot * SLOT + SLOT] = two.reshape(groups * 32, SLOT).astype(jnp.bfloat16)

    between[0].wait_recv()
    onward[0].start()
    place(0, pieces[0, pair], pieces[1, pair])
    for copy in beside:
        copy.wait_recv()
    place(1, pieces_in[0, 0], pieces_in[1, 0])
    between[1].wait_recv()
    onward[1].start()
    place(2, pieces_in[0, 1], pieces_in[1, 1])
    n_src = REACH * SRC
    for slot in range(4):
        for place_o in range(REACH):
            send(mine, sources_in.at[slot, place_o], src_s.at[0, 0], src_r.at[slot, place_o], chan_at(1), tm).wait_recv()
        block = sources_in[slot].astype(jnp.float32)
        joined = jnp.concatenate([block[:, :SRC, :], block[:, SRC:, :]], axis=2).reshape(n_src, length)
        padded[:, slot * SLOT : slot * SLOT + SLOT] = jnp.concatenate(
            [joined, jnp.zeros((n_src, SLOT - length), jnp.float32)], axis=1
        )
    for copy in onward:
        copy.wait_recv()
    place(3, pieces_in[0, 2], pieces_in[1, 2])

    scale = 1.0 / float(length * n_tm) ** 0.5

    def partial_copy(chunk, delta):
        first, last = CHUNKS[chunk]
        to = lax.rem(group + delta, groups)
        part = pl.ds(first, last - first)
        return send(
            partial.at[to, part], partial_in.at[delta - 1, part],
            part_s.at[chunk, delta - 1], part_r.at[chunk, delta - 1], chan, cousin(delta),
        )

    def product(shifts):
        wide = padded[...]
        shifted = jnp.concatenate([pltpu.roll(wide, c, 1) if c else wide for c in shifts], axis=0)
        result = lax.dot_general(
            lagged[...], shifted.astype(jnp.bfloat16), (((1,), (1,)), ((), ())),
            preferred_element_type=jnp.float32,
        )
        return (result * scale).reshape(groups, 2, 16, len(shifts) * n_src)

    for step in range(4):
        if step < 3:
            result = product(range(8 * step, 8 * step + 8)).astype(jnp.bfloat16)
            for late in range(2):
                for side in range(2):
                    partial[:, 4 * step + 2 * late + side] = result[:, late, :, side * 128 : side * 128 + 128]
        else:
            result = product(range(24, 26))
            partial[:, 12] = jnp.concatenate([result[:, 0], result[:, 1]], axis=2).astype(jnp.bfloat16)
        for chunk, (first, last) in enumerate(CHUNKS):
            if last == min(4 * step + 4, TILES):
                for delta in FAR_FIRST:
                    partial_copy(chunk, delta).start()

    tall = 512
    k = lax.broadcasted_iota(jnp.int32, (tall, tall), 0)
    j = lax.broadcasted_iota(jnp.int32, (tall, tall), 1)
    b = jnp.bitwise_and(k, 7)
    tile = jnp.bitwise_and(jnp.right_shift(k, 3), 15)
    quarter = jnp.right_shift(k, 7)
    mixed = tile == 12
    late = jnp.where(mixed, jnp.right_shift(quarter, 1), jnp.bitwise_and(jnp.right_shift(tile, 1), 1))
    shift = jnp.where(
        mixed, 24 + jnp.bitwise_and(quarter, 1),
        8 * jnp.right_shift(tile, 2) + 4 * jnp.bitwise_and(tile, 1) + quarter,
    )
    lag = shift - LATE * late + MAXLAG
    fits = jnp.logical_and(jnp.logical_and(lag >= 0, tile < TILES), b * LAGS + lag == j)
    order = fits.astype(jnp.float32).astype(jnp.bfloat16)

    for chunk in range(len(CHUNKS)):
        for delta in range(1, groups):
            partial_copy(chunk, delta).wait_recv()
    total = partial[group].astype(jnp.float32)
    for delta in range(1, groups):
        total = total + partial_in[delta - 1].astype(jnp.float32)
    spare = jnp.zeros((24, 128), jnp.float32)
    stack = []
    for owner in range(2):
        stack += [total[:, owner * 8 : owner * 8 + 8, :].reshape(TILES * 8, 128), spare]
    turned = jnp.concatenate(stack, axis=0).T
    flat = jnp.concatenate(
        [
            jnp.concatenate(
                [turned[n_src * s : n_src * s + n_src, owner * 128 : owner * 128 + 128] for s in range(4)], axis=1
            )
            for owner in range(2)
        ],
        axis=0,
    )
    high, low = split(flat)
    moved = jnp.dot(jnp.concatenate([high, low], axis=0), order, preferred_element_type=jnp.float32)
    sums[...] = moved[: 2 * n_src] + moved[2 * n_src :]

    sum_sends = []
    for place_o in range(REACH):
        low_d, high_d = OFFSETS[place_o], OFFSETS[REACH + place_o]
        back = chan_at(-low_d - core * (high_d - low_d))
        for owner in range(2):
            o = PLACES[place_o] + core * (PLACES[REACH + place_o] - PLACES[place_o])
            sum_sends.append(
                send(
                    sums.at[pl.ds((owner * REACH + place_o) * SRC, SRC), :], stacked.at[o],
                    sum_s.at[owner, place_o], sum_r.at[o], back, group * 4 + pair * 2 + owner,
                )
            )
            sum_sends[-1].start()
    for o in range(2 * REACH):
        send(sums.at[pl.ds(0, SRC), :], stacked.at[o], sum_s.at[0, 0], sum_r.at[o], chan_at(1), tm).wait_recv()
    out_ref[...] = stacked[...]

    to_right.wait_send()
    to_left.wait_send()
    for copy in source_sends + beside + between + onward + sum_sends:
        copy.wait_send()
    for chunk in range(len(CHUNKS)):
        for delta in range(1, groups):
            partial_copy(chunk, delta).wait_send()


def body(sizes, strain_rate):
    rows, length = strain_rate.shape
    n_chan, n_tm = sizes
    groups = n_tm // 4
    n_off = len(OFFSETS)
    f32, bf16 = jnp.float32, jnp.bfloat16
    dma = pltpu.SemaphoreType.DMA
    stacks = pl.pallas_call(
        functools.partial(correlate_kernel, sizes),
        out_shape=jax.ShapeDtypeStruct((n_off, SRC, 512), f32),
        in_specs=[pl.BlockSpec(memory_space=pl.ANY)],
        out_specs=pl.BlockSpec(memory_space=pltpu.VMEM),
        scratch_shapes=[
            pltpu.VMEM((rows, length), f32),
            pltpu.VMEM((2, rows // 2, EDGE), bf16),
            pltpu.VMEM((2, rows // 2, EDGE), bf16),
            pltpu.VMEM((rows, length), f32),
            pltpu.VMEM((2, 2, rows // 2, length // 2), bf16),
            pltpu.VMEM((2, 3, rows // 2, length // 2), bf16),
            pltpu.VMEM((2 * SRC, length // 2), bf16),
            pltpu.VMEM((4, REACH, 2 * SRC, length // 2), bf16),
            pltpu.VMEM((groups * 32, 4 * SLOT), bf16),
            pltpu.VMEM((REACH * SRC, 4 * SLOT), f32),
            pltpu.VMEM((groups, TILES, 16, 128), bf16),
            pltpu.VMEM((groups - 1, TILES, 16, 128), bf16),
            pltpu.VMEM((2 * REACH * SRC, 512), f32),
            pltpu.VMEM((n_off, SRC, 512), f32),
            dma, pltpu.SemaphoreType.REGULAR, dma((2,)), dma((2,)), dma((6,)), dma((6,)),
            dma((2, n_off)), dma((4, REACH)),
            dma((len(CHUNKS), groups - 1)), dma((len(CHUNKS), groups - 1)),
            dma((2, REACH)), dma((n_off,)),
        ],
        compiler_params=pltpu.CompilerParams(
            collective_id=0, has_side_effects=True, vmem_limit_bytes=55000 * 1024
        ),
    )(strain_rate)
    return jnp.transpose(stacks[:, :, : (rows // n_tm) * LAGS], (1, 0, 2))


def solution(mesh):
    sizes = (mesh.shape["chan"], mesh.shape["tm"])
    return jax.shard_map(
        functools.partial(body, sizes), mesh=mesh, in_specs=(P("chan", "tm"),),
        out_specs=P("chan", None, "tm"), check_vma=False,
    )
```

```python
import functools

import jax
import jax.numpy as jnp
from jax import lax
from jax.experimental import pallas as pl
from jax.experimental.pallas import tpu as pltpu
from jax.sharding import PartitionSpec as P

SRC = 8
MAXLAG = 25
LAGS = 51
W2 = 64
EDGE = 128
LATE = 26
SLOT = 640
REACH = 4
OFFSETS = (-4, 3, -2, 1, 4, -3, 2, -1)
PLACES = tuple(d + REACH if d < 0 else d + REACH - 1 for d in OFFSETS)
TILES = 13
FAR_FIRST = (4, 3, 5, 2, 6, 1, 7)
CHUNKS = ((0, 4), (4, 8), (8, 13))
MESH = pl.DeviceIdType.MESH


def split(value):
    high = value.astype(jnp.bfloat16)
    low = (value - high.astype(jnp.float32)).astype(jnp.bfloat16)
    return high, low


def correlate_kernel(
    sizes, x_hbm, out_ref,
    own, edges, halo, normed, pieces, pieces_in, mine, sources_in, lagged, padded, partial,
    partial_in, sums, stacked,
    load_sem, ready, halo_s, halo_r, piece_s, piece_r, src_s, src_r, part_s, part_r, sum_s, sum_r,
):
    n_chan, n_tm = sizes
    rows, length = own.shape
    groups = n_tm // 4
    chan = lax.axis_index("chan")
    tm = lax.axis_index("tm")
    group, pair, core = tm // 4, (tm // 2) % 2, tm % 2

    def chan_at(d):
        return lax.rem(chan + d + n_chan, n_chan)

    def tm_at(d):
        return lax.rem(tm + d + n_tm, n_tm)

    def mate(across, other):
        return group * 4 + lax.rem(pair + across, 2) * 2 + lax.rem(core + other, 2)

    def cousin(delta):
        return lax.rem(group + delta, groups) * 4 + pair * 2 + core

    mates = ((0, 1), (1, 0), (1, 1))

    load = pltpu.make_async_copy(x_hbm, own, load_sem)
    load.start()

    barrier = pltpu.get_barrier_semaphore()

    def greet(c, t):
        pl.semaphore_signal(barrier, inc=1, device_id=(c, t), device_id_type=MESH)

    greet(chan, tm_at(1))
    greet(chan, tm_at(-1))
    for d in OFFSETS:
        greet(chan_at(d), tm)
    for across, other in mates:
        greet(chan, mate(across, other))
    for delta in range(1, groups):
        greet(chan, cousin(delta))

    load.wait()
    value = own[...]
    half = rows // 2
    lane = lax.broadcasted_iota(jnp.int32, (half, EDGE), 1)
    first_edge = jnp.abs(value[:, :EDGE])
    last_edge = jnp.abs(value[:, length - EDGE :])
    edges[0] = jnp.where(lane < W2, pltpu.roll(last_edge[:half], W2, 1), last_edge[half:]).astype(jnp.bfloat16)
    edges[1] = jnp.where(lane < W2, first_edge[:half], pltpu.roll(first_edge[half:], W2, 1)).astype(jnp.bfloat16)
    row = lax.broadcasted_iota(jnp.int32, (512, 256), 0)
    col = lax.broadcasted_iota(jnp.int32, (512, 256), 1)
    band = (jnp.abs(row - EDGE - col) <= W2).astype(jnp.float32).astype(jnp.bfloat16)

    pl.semaphore_wait(barrier, 2 + len(OFFSETS) + len(mates) + groups - 1)

    def send(src, dst, s, r, c, t):
        return pltpu.make_async_remote_copy(
            src_ref=src, dst_ref=dst, send_sem=s, recv_sem=r,
            device_id=(c, t), device_id_type=MESH,
        )

    to_right = send(edges.at[0], halo.at[0], halo_s.at[0], halo_r.at[0], chan, tm_at(1))
    to_left = send(edges.at[1], halo.at[1], halo_s.at[1], halo_r.at[1], chan, tm_at(-1))
    to_right.start()
    to_left.start()
    for across, other in mates:
        pl.semaphore_signal(ready, inc=1, device_id=(chan, mate(across, other)), device_id_type=MESH)

    def normalise(window, here):
        high, low = split(window)
        total = jnp.dot(
            jnp.concatenate([high, low], axis=0), band[: window.shape[1], : here.stop - here.start],
            preferred_element_type=jnp.float32,
        )
        level = (total[:rows] + total[rows:]) / (2 * W2 + 1) + 1e-05
        normed[:, here] = (value[:, here] / level).astype(jnp.bfloat16).astype(jnp.float32)

    def piece_send(src, kind, slot, across, other):
        n = 2 * slot + kind
        return send(src, pieces_in.at[kind, slot], piece_s.at[n], piece_r.at[n], chan, mate(across, other))

    beside = [piece_send(pieces.at[kind, pair], kind, 0, 0, 1) for kind in range(2)]
    between = [piece_send(pieces.at[kind, 1 - pair], kind, 1, 1, 0) for kind in range(2)]
    onward = [piece_send(pieces_in.at[kind, 1], kind, 2, 0, 1) for kind in range(2)]

    def give_pieces(kind):
        for p in range(2):
            for g in range(groups):
                at = pl.ds(g * 32 + p * 16, 16)
                if kind == 0:
                    block = normed[at, EDGE : length - EDGE]
                else:
                    block = jnp.concatenate([normed[at, :EDGE], normed[at, length - EDGE :]], axis=1)
                pieces[kind, p, pl.ds(g * 16, 16), :] = block.astype(jnp.bfloat16)
        between[kind].start()
        beside[kind].start()

    source_sends = []

    def give_sources(kind):
        picked = []
        for q in range(SRC):
            at = pl.ds(q * (rows // SRC), 1)
            if kind == 0:
                picked.append(normed[at, EDGE : length - EDGE])
            else:
                picked.append(jnp.concatenate([normed[at, :EDGE], normed[at, length - EDGE :]], axis=1))
        block = jnp.concatenate(picked, axis=0)
        mine[kind] = jnp.concatenate([block[:, :EDGE], block[:, EDGE:]], axis=0).astype(jnp.bfloat16)
        for across in range(2):
            for o, d in enumerate(OFFSETS):
                side, place_o = o // REACH, o % REACH
                slot = across * 2 + lax.rem(core + side, 2)
                to = group * 4 + lax.rem(pair + across, 2) * 2 + side
                source_sends.append(
                    send(
                        mine.at[kind], sources_in.at[kind, slot, place_o], src_s.at[kind, across, o],
                        src_r.at[kind, slot, place_o], chan_at(d), to,
                    )
                )
                source_sends[-1].start()

    absolute = jnp.abs(value)
    normalise(absolute, slice(EDGE, length - EDGE))
    pl.semaphore_wait(ready, len(mates))
    give_sources(0)
    give_pieces(0)

    to_right.wait_recv()
    to_left.wait_recv()
    before = halo[0].astype(jnp.float32) * (tm > 0).astype(jnp.float32)
    after = halo[1].astype(jnp.float32) * (tm < n_tm - 1).astype(jnp.float32)
    left = jnp.concatenate([pltpu.roll(before, W2, 1), before], axis=0)
    right = jnp.concatenate([after, pltpu.roll(after, W2, 1)], axis=0)
    normalise(jnp.concatenate([left, absolute[:, : 2 * EDGE]], axis=1), slice(0, EDGE))
    normalise(jnp.concatenate([absolute[:, length - 2 * EDGE :], right], axis=1), slice(length - EDGE, length))

    give_pieces(1)
    give_sources(1)

    count = groups * 16
    blank = jnp.zeros((count, SLOT - length), jnp.float32)

    def place(slot, middle, ends):
        middle, ends = middle.astype(jnp.float32), ends.astype(jnp.float32)
        wide = jnp.concatenate([ends[:, :EDGE], middle, ends[:, EDGE:], blank], axis=1)
        late = pltpu.roll(wide, LATE, 1)
        two = jnp.concatenate([wide.reshape(groups, 16, SLOT), late.reshape(groups, 16, SLOT)], axis=1)
        lagged[:, slot * SLOT : slot * SLOT + SLOT] = two.reshape(groups * 32, SLOT).astype(jnp.bfloat16)

    between[0].wait_recv()
    onward[0].start()
    place(0, pieces[0, pair], pieces[1, pair])
    for copy in beside:
        copy.wait_recv()
    place(1, pieces_in[0, 0], pieces_in[1, 0])
    between[1].wait_recv()
    onward[1].start()
    place(2, pieces_in[0, 1], pieces_in[1, 1])
    n_src = REACH * SRC
    for slot in range(4):
        for kind in range(2):
            for place_o in range(REACH):
                send(
                    mine.at[0], sources_in.at[kind, slot, place_o], src_s.at[0, 0, 0],
                    src_r.at[kind, slot, place_o], chan_at(1), tm,
                ).wait_recv()
        middle, ends = [sources_in[kind, slot].astype(jnp.float32) for kind in range(2)]
        joined = jnp.concatenate(
            [ends[:, :SRC], middle[:, :SRC], middle[:, SRC:], ends[:, SRC:]], axis=2
        ).reshape(n_src, length)
        padded[:, slot * SLOT : slot * SLOT + SLOT] = jnp.concatenate(
            [joined, jnp.zeros((n_src, SLOT - length), jnp.float32)], axis=1
        )
    for copy in onward:
        copy.wait_recv()
    place(3, pieces_in[0, 2], pieces_in[1, 2])

    scale = 1.0 / float(length * n_tm) ** 0.5

    def partial_copy(chunk, delta):
        first, last = CHUNKS[chunk]
        to = lax.rem(group + delta, groups)
        part = pl.ds(first, last - first)
        return send(
            partial.at[to, part], partial_in.at[delta - 1, part],
            part_s.at[chunk, delta - 1], part_r.at[chunk, delta - 1], chan, cousin(delta),
        )

    def product(shifts):
        wide = padded[...]
        shifted = jnp.concatenate([pltpu.roll(wide, c, 1) if c else wide for c in shifts], axis=0)
        result = lax.dot_general(
            lagged[...], shifted.astype(jnp.bfloat16), (((1,), (1,)), ((), ())),
            preferred_element_type=jnp.float32,
        )
        return (result * scale).reshape(groups, 2, 16, len(shifts) * n_src)

    for step in range(4):
        if step < 3:
            result = product(range(8 * step, 8 * step + 8)).astype(jnp.bfloat16)
            for late in range(2):
                for side in range(2):
                    partial[:, 4 * step + 2 * late + side] = result[:, late, :, side * 128 : side * 128 + 128]
        else:
            result = product(range(24, 26))
            partial[:, 12] = jnp.concatenate([result[:, 0], result[:, 1]], axis=2).astype(jnp.bfloat16)
        for chunk, (first, last) in enumerate(CHUNKS):
            if last == min(4 * step + 4, TILES):
                for delta in FAR_FIRST:
                    partial_copy(chunk, delta).start()

    tall = 512
    k = lax.broadcasted_iota(jnp.int32, (tall, tall), 0)
    j = lax.broadcasted_iota(jnp.int32, (tall, tall), 1)
    b = jnp.bitwise_and(k, 7)
    tile = jnp.bitwise_and(jnp.right_shift(k, 3), 15)
    quarter = jnp.right_shift(k, 7)
    mixed = tile == 12
    late = jnp.where(mixed, jnp.right_shift(quarter, 1), jnp.bitwise_and(jnp.right_shift(tile, 1), 1))
    shift = jnp.where(
        mixed, 24 + jnp.bitwise_and(quarter, 1),
        8 * jnp.right_shift(tile, 2) + 4 * jnp.bitwise_and(tile, 1) + quarter,
    )
    lag = shift - LATE * late + MAXLAG
    fits = jnp.logical_and(jnp.logical_and(lag >= 0, tile < TILES), b * LAGS + lag == j)
    order = fits.astype(jnp.float32).astype(jnp.bfloat16)

    total = partial[group].astype(jnp.float32)
    for delta in FAR_FIRST[::-1]:
        for chunk in range(len(CHUNKS)):
            partial_copy(chunk, delta).wait_recv()
        total = total + partial_in[delta - 1].astype(jnp.float32)
    spare = jnp.zeros((24, 128), jnp.float32)
    stack = []
    for owner in range(2):
        stack += [total[:, owner * 8 : owner * 8 + 8, :].reshape(TILES * 8, 128), spare]
    turned = jnp.concatenate(stack, axis=0).T
    flat = jnp.concatenate(
        [
            jnp.concatenate(
                [turned[n_src * s : n_src * s + n_src, owner * 128 : owner * 128 + 128] for s in range(4)], axis=1
            )
            for owner in range(2)
        ],
        axis=0,
    )
    high, low = split(flat)
    moved = jnp.dot(jnp.concatenate([high, low], axis=0), order, preferred_element_type=jnp.float32)
    sums[...] = moved[: 2 * n_src] + moved[2 * n_src :]

    sum_sends = []
    for place_o in range(REACH):
        low_d, high_d = OFFSETS[place_o], OFFSETS[REACH + place_o]
        back = chan_at(-low_d - core * (high_d - low_d))
        for owner in range(2):
            o = PLACES[place_o] + core * (PLACES[REACH + place_o] - PLACES[place_o])
            sum_sends.append(
                send(
                    sums.at[pl.ds((owner * REACH + place_o) * SRC, SRC), :], stacked.at[o],
                    sum_s.at[owner, place_o], sum_r.at[o], back, group * 4 + pair * 2 + owner,
                )
            )
            sum_sends[-1].start()
    for o in range(2 * REACH):
        send(sums.at[pl.ds(0, SRC), :], stacked.at[o], sum_s.at[0, 0], sum_r.at[o], chan_at(1), tm).wait_recv()
    out_ref[...] = stacked[...]

    to_right.wait_send()
    to_left.wait_send()
    for copy in source_sends + beside + between + onward + sum_sends:
        copy.wait_send()
    for chunk in range(len(CHUNKS)):
        for delta in range(1, groups):
            partial_copy(chunk, delta).wait_send()


def body(sizes, strain_rate):
    rows, length = strain_rate.shape
    n_chan, n_tm = sizes
    groups = n_tm // 4
    n_off = len(OFFSETS)
    f32, bf16 = jnp.float32, jnp.bfloat16
    dma = pltpu.SemaphoreType.DMA
    stacks = pl.pallas_call(
        functools.partial(correlate_kernel, sizes),
        out_shape=jax.ShapeDtypeStruct((n_off, SRC, 512), f32),
        in_specs=[pl.BlockSpec(memory_space=pl.ANY)],
        out_specs=pl.BlockSpec(memory_space=pltpu.VMEM),
        scratch_shapes=[
            pltpu.VMEM((rows, length), f32),
            pltpu.VMEM((2, rows // 2, EDGE), bf16),
            pltpu.VMEM((2, rows // 2, EDGE), bf16),
            pltpu.VMEM((rows, length), f32),
            pltpu.VMEM((2, 2, rows // 2, length // 2), bf16),
            pltpu.VMEM((2, 3, rows // 2, length // 2), bf16),
            pltpu.VMEM((2, 2 * SRC, EDGE), bf16),
            pltpu.VMEM((2, 4, REACH, 2 * SRC, EDGE), bf16),
            pltpu.VMEM((groups * 32, 4 * SLOT), bf16),
            pltpu.VMEM((REACH * SRC, 4 * SLOT), f32),
            pltpu.VMEM((groups, TILES, 16, 128), bf16),
            pltpu.VMEM((groups - 1, TILES, 16, 128), bf16),
            pltpu.VMEM((2 * REACH * SRC, 512), f32),
            pltpu.VMEM((n_off, SRC, 512), f32),
            dma, pltpu.SemaphoreType.REGULAR, dma((2,)), dma((2,)), dma((6,)), dma((6,)),
            dma((2, 2, n_off)), dma((2, 4, REACH)),
            dma((len(CHUNKS), groups - 1)), dma((len(CHUNKS), groups - 1)),
            dma((2, REACH)), dma((n_off,)),
        ],
        compiler_params=pltpu.CompilerParams(
            collective_id=0, has_side_effects=True, vmem_limit_bytes=55000 * 1024
        ),
    )(strain_rate)
    return jnp.transpose(stacks[:, :, : (rows // n_tm) * LAGS], (1, 0, 2))


def solution(mesh):
    sizes = (mesh.shape["chan"], mesh.shape["tm"])
    return jax.shard_map(
        functools.partial(body, sizes), mesh=mesh, in_specs=(P("chan", "tm"),),
        out_specs=P("chan", None, "tm"), check_vma=False,
    )
```

```python
import functools

import jax
import jax.numpy as jnp
from jax import lax
from jax.experimental import pallas as pl
from jax.experimental.pallas import tpu as pltpu
from jax.sharding import PartitionSpec as P

SRC = 8
MAXLAG = 25
LAGS = 51
W2 = 64
EDGE = 128
LATE = 26
SLOT = 640
REACH = 4
OFFSETS = (-4, 3, -2, 1, 4, -3, 2, -1)
PLACES = tuple(d + REACH if d < 0 else d + REACH - 1 for d in OFFSETS)
TILES = 13
FAR_FIRST = (4, 3, 5, 2, 6, 1, 7)
CHUNKS = ((0, 4), (4, 8), (8, 13))
MESH = pl.DeviceIdType.MESH


def split(value):
    high = value.astype(jnp.bfloat16)
    low = (value - high.astype(jnp.float32)).astype(jnp.bfloat16)
    return high, low


def correlate_kernel(
    sizes, x_hbm, out_ref,
    own, edges, halo, normed, pieces, pieces_in, mine, sources_in, lagged, padded, partial,
    partial_in, sums, stacked,
    load_sem, ready, halo_s, halo_r, piece_s, piece_r, src_s, src_r, part_s, part_r, sum_s, sum_r,
):
    n_chan, n_tm = sizes
    rows, length = own.shape
    groups = n_tm // 4
    chan = lax.axis_index("chan")
    tm = lax.axis_index("tm")
    group, pair, core = tm // 4, (tm // 2) % 2, tm % 2

    def chan_at(d):
        return lax.rem(chan + d + n_chan, n_chan)

    def tm_at(d):
        return lax.rem(tm + d + n_tm, n_tm)

    def mate(across, other):
        return group * 4 + lax.rem(pair + across, 2) * 2 + lax.rem(core + other, 2)

    def cousin(delta):
        return lax.rem(group + delta, groups) * 4 + pair * 2 + core

    mates = ((0, 1), (1, 0), (1, 1))

    load = pltpu.make_async_copy(x_hbm, own, load_sem)
    load.start()

    barrier = pltpu.get_barrier_semaphore()

    def greet(c, t):
        pl.semaphore_signal(barrier, inc=1, device_id=(c, t), device_id_type=MESH)

    greet(chan, tm_at(1))
    greet(chan, tm_at(-1))
    for d in OFFSETS:
        greet(chan_at(d), tm)
    for across, other in mates:
        greet(chan, mate(across, other))
    for delta in range(1, groups):
        greet(chan, cousin(delta))

    load.wait()
    value = own[...]
    half = rows // 2
    lane = lax.broadcasted_iota(jnp.int32, (half, EDGE), 1)
    first_edge = jnp.abs(value[:, :EDGE])
    last_edge = jnp.abs(value[:, length - EDGE :])
    edges[0] = jnp.where(lane < W2, pltpu.roll(last_edge[:half], W2, 1), last_edge[half:]).astype(jnp.bfloat16)
    edges[1] = jnp.where(lane < W2, first_edge[:half], pltpu.roll(first_edge[half:], W2, 1)).astype(jnp.bfloat16)
    row = lax.broadcasted_iota(jnp.int32, (512, 256), 0)
    col = lax.broadcasted_iota(jnp.int32, (512, 256), 1)
    band = (jnp.abs(row - EDGE - col) <= W2).astype(jnp.float32).astype(jnp.bfloat16)

    pl.semaphore_wait(barrier, 2 + len(OFFSETS) + len(mates) + groups - 1)

    def send(src, dst, s, r, c, t):
        return pltpu.make_async_remote_copy(
            src_ref=src, dst_ref=dst, send_sem=s, recv_sem=r,
            device_id=(c, t), device_id_type=MESH,
        )

    to_right = send(edges.at[0], halo.at[0], halo_s.at[0], halo_r.at[0], chan, tm_at(1))
    to_left = send(edges.at[1], halo.at[1], halo_s.at[1], halo_r.at[1], chan, tm_at(-1))
    to_right.start()
    to_left.start()
    for across, other in mates:
        pl.semaphore_signal(ready, inc=1, device_id=(chan, mate(across, other)), device_id_type=MESH)

    def normalise(window, here):
        high, low = split(window)
        total = jnp.dot(
            jnp.concatenate([high, low], axis=0), band[: window.shape[1], : here.stop - here.start],
            preferred_element_type=jnp.float32,
        )
        level = (total[:rows] + total[rows:]) / (2 * W2 + 1) + 1e-05
        normed[:, here] = (value[:, here] / level).astype(jnp.bfloat16).astype(jnp.float32)

    def piece_send(src, kind, slot, across, other):
        n = 2 * slot + kind
        return send(src, pieces_in.at[kind, slot], piece_s.at[n], piece_r.at[n], chan, mate(across, other))

    beside = [piece_send(pieces.at[kind, pair], kind, 0, 0, 1) for kind in range(2)]
    between = [piece_send(pieces.at[kind, 1 - pair], kind, 1, 1, 0) for kind in range(2)]
    onward = [piece_send(pieces_in.at[kind, 1], kind, 2, 0, 1) for kind in range(2)]

    def give_pieces(kind):
        for p in range(2):
            for g in range(groups):
                at = pl.ds(g * 32 + p * 16, 16)
                if kind == 0:
                    block = normed[at, EDGE : length - EDGE]
                else:
                    block = jnp.concatenate([normed[at, :EDGE], normed[at, length - EDGE :]], axis=1)
                pieces[kind, p, pl.ds(g * 16, 16), :] = block.astype(jnp.bfloat16)
        between[kind].start()
        beside[kind].start()

    source_sends = []

    def give_sources(kind):
        picked = []
        for q in range(SRC):
            at = pl.ds(q * (rows // SRC), 1)
            if kind == 0:
                picked.append(normed[at, EDGE : length - EDGE])
            else:
                picked.append(jnp.concatenate([normed[at, :EDGE], normed[at, length - EDGE :]], axis=1))
        block = jnp.concatenate(picked, axis=0)
        mine[kind] = jnp.concatenate([block[:, :EDGE], block[:, EDGE:]], axis=0).astype(jnp.bfloat16)
        for across in range(2):
            for o, d in enumerate(OFFSETS):
                side, place_o = o // REACH, o % REACH
                slot = across * 2 + lax.rem(core + side, 2)
                to = group * 4 + lax.rem(pair + across, 2) * 2 + side
                source_sends.append(
                    send(
                        mine.at[kind], sources_in.at[kind, slot, place_o], src_s.at[kind, across, o],
                        src_r.at[kind, slot, place_o], chan_at(d), to,
                    )
                )
                source_sends[-1].start()

    absolute = jnp.abs(value)
    normalise(absolute, slice(EDGE, length - EDGE))
    pl.semaphore_wait(ready, len(mates))
    give_sources(0)
    give_pieces(0)

    to_right.wait_recv()
    to_left.wait_recv()
    before = halo[0].astype(jnp.float32) * (tm > 0).astype(jnp.float32)
    after = halo[1].astype(jnp.float32) * (tm < n_tm - 1).astype(jnp.float32)
    left = jnp.concatenate([pltpu.roll(before, W2, 1), before], axis=0)
    right = jnp.concatenate([after, pltpu.roll(after, W2, 1)], axis=0)
    normalise(jnp.concatenate([left, absolute[:, : 2 * EDGE]], axis=1), slice(0, EDGE))
    normalise(jnp.concatenate([absolute[:, length - 2 * EDGE :], right], axis=1), slice(length - EDGE, length))

    give_pieces(1)
    give_sources(1)

    count = groups * 16
    blank = jnp.zeros((count, SLOT - length), jnp.float32)

    def place(slot, middle, ends):
        middle, ends = middle.astype(jnp.float32), ends.astype(jnp.float32)
        wide = jnp.concatenate([ends[:, :EDGE], middle, ends[:, EDGE:], blank], axis=1)
        late = pltpu.roll(wide, LATE, 1)
        two = jnp.concatenate([wide.reshape(groups, 16, SLOT), late.reshape(groups, 16, SLOT)], axis=1)
        lagged[:, slot * SLOT : slot * SLOT + SLOT] = two.reshape(groups * 32, SLOT).astype(jnp.bfloat16)

    between[0].wait_recv()
    onward[0].start()
    place(0, pieces[0, pair], pieces[1, pair])
    for copy in beside:
        copy.wait_recv()
    place(1, pieces_in[0, 0], pieces_in[1, 0])
    between[1].wait_recv()
    onward[1].start()
    place(2, pieces_in[0, 1], pieces_in[1, 1])
    n_src = REACH * SRC
    for slot in range(4):
        for kind in range(2):
            for place_o in range(REACH):
                send(
                    mine.at[0], sources_in.at[kind, slot, place_o], src_s.at[0, 0, 0],
                    src_r.at[kind, slot, place_o], chan_at(1), tm,
                ).wait_recv()
        middle, ends = [sources_in[kind, slot].astype(jnp.float32) for kind in range(2)]
        joined = jnp.concatenate(
            [ends[:, :SRC], middle[:, :SRC], middle[:, SRC:], ends[:, SRC:]], axis=2
        ).reshape(n_src, length)
        padded[:, slot * SLOT : slot * SLOT + SLOT] = jnp.concatenate(
            [joined, jnp.zeros((n_src, SLOT - length), jnp.float32)], axis=1
        )
    for copy in onward:
        copy.wait_recv()
    place(3, pieces_in[0, 2], pieces_in[1, 2])

    scale = 1.0 / float(length * n_tm) ** 0.5

    def partial_copy(chunk, delta):
        first, last = CHUNKS[chunk]
        to = lax.rem(group + delta, groups)
        part = pl.ds(first, last - first)
        return send(
            partial.at[to, part], partial_in.at[delta - 1, part],
            part_s.at[chunk, delta - 1], part_r.at[chunk, delta - 1], chan, cousin(delta),
        )

    def product(shifts):
        wide = padded[...]
        shifted = jnp.concatenate([pltpu.roll(wide, c, 1) if c else wide for c in shifts], axis=0)
        result = lax.dot_general(
            lagged[...], shifted.astype(jnp.bfloat16), (((1,), (1,)), ((), ())),
            preferred_element_type=jnp.float32,
        )
        return (result * scale).reshape(groups, 2, 16, len(shifts) * n_src)

    for step in range(4):
        if step < 3:
            result = product(range(8 * step, 8 * step + 8)).astype(jnp.bfloat16)
            for late in range(2):
                for side in range(2):
                    partial[:, 4 * step + 2 * late + side] = result[:, late, :, side * 128 : side * 128 + 128]
        else:
            result = product(range(24, 26))
            partial[:, 12] = jnp.concatenate([result[:, 0], result[:, 1]], axis=2).astype(jnp.bfloat16)
        for chunk, (first, last) in enumerate(CHUNKS):
            if last == min(4 * step + 4, TILES):
                for delta in FAR_FIRST:
                    partial_copy(chunk, delta).start()

    tall = 512
    k = lax.broadcasted_iota(jnp.int32, (tall, tall), 0)
    j = lax.broadcasted_iota(jnp.int32, (tall, tall), 1)
    b = jnp.bitwise_and(k, 7)
    tile = jnp.bitwise_and(jnp.right_shift(k, 3), 15)
    quarter = jnp.right_shift(k, 7)
    mixed = tile == 12
    late = jnp.where(mixed, jnp.right_shift(quarter, 1), jnp.bitwise_and(jnp.right_shift(tile, 1), 1))
    shift = jnp.where(
        mixed, 24 + jnp.bitwise_and(quarter, 1),
        8 * jnp.right_shift(tile, 2) + 4 * jnp.bitwise_and(tile, 1) + quarter,
    )
    lag = shift - LATE * late + MAXLAG
    fits = jnp.logical_and(jnp.logical_and(lag >= 0, tile < TILES), b * LAGS + lag == j)
    order = fits.astype(jnp.float32).astype(jnp.bfloat16)

    total = partial[group].astype(jnp.float32)
    for delta in FAR_FIRST[::-1]:
        for chunk in range(len(CHUNKS)):
            partial_copy(chunk, delta).wait_recv()
        total = total + partial_in[delta - 1].astype(jnp.float32)
    spare = jnp.zeros((24, 128), jnp.float32)
    stack = []
    for owner in range(2):
        stack += [total[:, owner * 8 : owner * 8 + 8, :].reshape(TILES * 8, 128), spare]
    turned = jnp.concatenate(stack, axis=0).T
    flat = jnp.concatenate(
        [
            jnp.concatenate(
                [turned[n_src * s : n_src * s + n_src, owner * 128 : owner * 128 + 128] for s in range(4)], axis=1
            )
            for owner in range(2)
        ],
        axis=0,
    )
    high, low = split(flat)
    moved = jnp.dot(jnp.concatenate([high, low], axis=0), order, preferred_element_type=jnp.float32)
    sums[...] = moved[: 2 * n_src] + moved[2 * n_src :]

    sum_sends = []
    for place_o in range(REACH):
        low_d, high_d = OFFSETS[place_o], OFFSETS[REACH + place_o]
        back = chan_at(-low_d - core * (high_d - low_d))
        for owner in range(2):
            o = PLACES[place_o] + core * (PLACES[REACH + place_o] - PLACES[place_o])
            sum_sends.append(
                send(
                    sums.at[pl.ds((owner * REACH + place_o) * SRC, SRC), :], stacked.at[o],
                    sum_s.at[owner, place_o], sum_r.at[o], back, group * 4 + pair * 2 + owner,
                )
            )
            sum_sends[-1].start()
    for o in range(2 * REACH):
        send(sums.at[pl.ds(0, SRC), :], stacked.at[o], sum_s.at[0, 0], sum_r.at[o], chan_at(1), tm).wait_recv()
    for q in range(SRC):
        out_ref[q] = stacked[:, q, :][:, : out_ref.shape[2]]

    to_right.wait_send()
    to_left.wait_send()
    for copy in source_sends + beside + between + onward + sum_sends:
        copy.wait_send()
    for chunk in range(len(CHUNKS)):
        for delta in range(1, groups):
            partial_copy(chunk, delta).wait_send()


def body(sizes, strain_rate):
    rows, length = strain_rate.shape
    n_chan, n_tm = sizes
    groups = n_tm // 4
    n_off = len(OFFSETS)
    f32, bf16 = jnp.float32, jnp.bfloat16
    dma = pltpu.SemaphoreType.DMA
    return pl.pallas_call(
        functools.partial(correlate_kernel, sizes),
        out_shape=jax.ShapeDtypeStruct((SRC, n_off, (rows // n_tm) * LAGS), f32),
        in_specs=[pl.BlockSpec(memory_space=pl.ANY)],
        out_specs=pl.BlockSpec(memory_space=pltpu.VMEM),
        scratch_shapes=[
            pltpu.VMEM((rows, length), f32),
            pltpu.VMEM((2, rows // 2, EDGE), bf16),
            pltpu.VMEM((2, rows // 2, EDGE), bf16),
            pltpu.VMEM((rows, length), f32),
            pltpu.VMEM((2, 2, rows // 2, length // 2), bf16),
            pltpu.VMEM((2, 3, rows // 2, length // 2), bf16),
            pltpu.VMEM((2, 2 * SRC, EDGE), bf16),
            pltpu.VMEM((2, 4, REACH, 2 * SRC, EDGE), bf16),
            pltpu.VMEM((groups * 32, 4 * SLOT), bf16),
            pltpu.VMEM((REACH * SRC, 4 * SLOT), f32),
            pltpu.VMEM((groups, TILES, 16, 128), bf16),
            pltpu.VMEM((groups - 1, TILES, 16, 128), bf16),
            pltpu.VMEM((2 * REACH * SRC, 512), f32),
            pltpu.VMEM((n_off, SRC, 512), f32),
            dma, pltpu.SemaphoreType.REGULAR, dma((2,)), dma((2,)), dma((6,)), dma((6,)),
            dma((2, 2, n_off)), dma((2, 4, REACH)),
            dma((len(CHUNKS), groups - 1)), dma((len(CHUNKS), groups - 1)),
            dma((2, REACH)), dma((n_off,)),
        ],
        compiler_params=pltpu.CompilerParams(
            collective_id=0, has_side_effects=True, vmem_limit_bytes=55000 * 1024
        ),
    )(strain_rate)


def solution(mesh):
    sizes = (mesh.shape["chan"], mesh.shape["tm"])
    return jax.shard_map(
        functools.partial(body, sizes), mesh=mesh, in_specs=(P("chan", "tm"),),
        out_specs=P("chan", None, "tm"), check_vma=False,
    )
```

```python
import functools

import jax
import jax.numpy as jnp
from jax import lax
from jax.experimental import pallas as pl
from jax.experimental.pallas import tpu as pltpu
from jax.sharding import PartitionSpec as P

SRC = 8
MAXLAG = 25
LAGS = 51
W2 = 64
EDGE = 128
LATE = 26
SLOT = 640
REACH = 4
OFFSETS = (-4, 3, -2, 1, 4, -3, 2, -1)
PLACES = tuple(d + REACH if d < 0 else d + REACH - 1 for d in OFFSETS)
TILES = 13
FAR_FIRST = (4, 3, 5, 2, 6, 1, 7)
CHUNKS = ((0, 4), (4, 8), (8, 13))
MESH = pl.DeviceIdType.MESH


def split(value):
    high = value.astype(jnp.bfloat16)
    low = (value - high.astype(jnp.float32)).astype(jnp.bfloat16)
    return high, low


def correlate_kernel(
    sizes, x_hbm, out_ref,
    own, edges, halo, normed, pieces, pieces_in, mine, sources_in, lagged, padded, partial,
    partial_in, sums, stacked,
    load_sem, ready, halo_s, halo_r, piece_s, piece_r, src_s, src_r, part_s, part_r, sum_s, sum_r,
):
    n_chan, n_tm = sizes
    rows, length = own.shape
    groups = n_tm // 4
    chan = lax.axis_index("chan")
    tm = lax.axis_index("tm")
    group, pair, core = tm // 4, (tm // 2) % 2, tm % 2

    def chan_at(d):
        return lax.rem(chan + d + n_chan, n_chan)

    def tm_at(d):
        return lax.rem(tm + d + n_tm, n_tm)

    def mate(across, other):
        return group * 4 + lax.rem(pair + across, 2) * 2 + lax.rem(core + other, 2)

    def cousin(delta):
        return lax.rem(group + delta, groups) * 4 + pair * 2 + core

    mates = ((0, 1), (1, 0), (1, 1))

    load = pltpu.make_async_copy(x_hbm, own, load_sem)
    load.start()

    barrier = pltpu.get_barrier_semaphore()

    def greet(c, t):
        pl.semaphore_signal(barrier, inc=1, device_id=(c, t), device_id_type=MESH)

    greet(chan, tm_at(1))
    greet(chan, tm_at(-1))
    for d in OFFSETS:
        greet(chan_at(d), tm)
    for across, other in mates:
        greet(chan, mate(across, other))
    for delta in range(1, groups):
        greet(chan, cousin(delta))

    load.wait()
    value = own[...]
    half = rows // 2
    lane = lax.broadcasted_iota(jnp.int32, (half, EDGE), 1)
    first_edge = jnp.abs(value[:, :EDGE])
    last_edge = jnp.abs(value[:, length - EDGE :])
    edges[0] = jnp.where(lane < W2, pltpu.roll(last_edge[:half], W2, 1), last_edge[half:]).astype(jnp.bfloat16)
    edges[1] = jnp.where(lane < W2, first_edge[:half], pltpu.roll(first_edge[half:], W2, 1)).astype(jnp.bfloat16)
    row = lax.broadcasted_iota(jnp.int32, (512, 256), 0)
    col = lax.broadcasted_iota(jnp.int32, (512, 256), 1)
    band = (jnp.abs(row - EDGE - col) <= W2).astype(jnp.float32).astype(jnp.bfloat16)

    def put(total, here):
        level = total / (2 * W2 + 1) + 1e-05
        normed[:, here] = (value[:, here] / level).astype(jnp.bfloat16).astype(jnp.float32)

    def summed(window, weights):
        total = jnp.dot(window, weights, preferred_element_type=jnp.float32)
        return total[:rows] + total[rows:]

    high, low = split(jnp.abs(value))
    both = jnp.concatenate([high, low], axis=0)
    put(summed(both, band), slice(EDGE, length - EDGE))
    total_first = summed(both[:, : 2 * EDGE], band[EDGE : 3 * EDGE, :EDGE])
    total_last = summed(both[:, length - 2 * EDGE :], band[: 2 * EDGE, :EDGE])

    pl.semaphore_wait(barrier, 2 + len(OFFSETS) + len(mates) + groups - 1)

    def send(src, dst, s, r, c, t):
        return pltpu.make_async_remote_copy(
            src_ref=src, dst_ref=dst, send_sem=s, recv_sem=r,
            device_id=(c, t), device_id_type=MESH,
        )

    to_right = send(edges.at[0], halo.at[0], halo_s.at[0], halo_r.at[0], chan, tm_at(1))
    to_left = send(edges.at[1], halo.at[1], halo_s.at[1], halo_r.at[1], chan, tm_at(-1))
    to_right.start()
    to_left.start()
    for across, other in mates:
        pl.semaphore_signal(ready, inc=1, device_id=(chan, mate(across, other)), device_id_type=MESH)

    def piece_send(src, kind, slot, across, other):
        n = 2 * slot + kind
        return send(src, pieces_in.at[kind, slot], piece_s.at[n], piece_r.at[n], chan, mate(across, other))

    beside = [piece_send(pieces.at[kind, pair], kind, 0, 0, 1) for kind in range(2)]
    between = [piece_send(pieces.at[kind, 1 - pair], kind, 1, 1, 0) for kind in range(2)]
    onward = [piece_send(pieces_in.at[kind, 1], kind, 2, 0, 1) for kind in range(2)]

    def give_pieces(kind):
        for p in range(2):
            for g in range(groups):
                at = pl.ds(g * 32 + p * 16, 16)
                if kind == 0:
                    block = normed[at, EDGE : length - EDGE]
                else:
                    block = jnp.concatenate([normed[at, :EDGE], normed[at, length - EDGE :]], axis=1)
                pieces[kind, p, pl.ds(g * 16, 16), :] = block.astype(jnp.bfloat16)
        between[kind].start()
        beside[kind].start()

    source_sends = []

    def give_sources(kind):
        picked = []
        for q in range(SRC):
            at = pl.ds(q * (rows // SRC), 1)
            if kind == 0:
                picked.append(normed[at, EDGE : length - EDGE])
            else:
                picked.append(jnp.concatenate([normed[at, :EDGE], normed[at, length - EDGE :]], axis=1))
        block = jnp.concatenate(picked, axis=0)
        mine[kind] = jnp.concatenate([block[:, :EDGE], block[:, EDGE:]], axis=0).astype(jnp.bfloat16)
        for across in range(2):
            for o, d in enumerate(OFFSETS):
                side, place_o = o // REACH, o % REACH
                slot = across * 2 + lax.rem(core + side, 2)
                to = group * 4 + lax.rem(pair + across, 2) * 2 + side
                source_sends.append(
                    send(
                        mine.at[kind], sources_in.at[kind, slot, place_o], src_s.at[kind, across, o],
                        src_r.at[kind, slot, place_o], chan_at(d), to,
                    )
                )
                source_sends[-1].start()

    pl.semaphore_wait(ready, len(mates))
    give_sources(0)
    give_pieces(0)

    to_right.wait_recv()
    to_left.wait_recv()
    before = halo[0].astype(jnp.float32) * (tm > 0).astype(jnp.float32)
    after = halo[1].astype(jnp.float32) * (tm < n_tm - 1).astype(jnp.float32)
    left = jnp.concatenate([pltpu.roll(before, W2, 1), before], axis=0).astype(jnp.bfloat16)
    right = jnp.concatenate([after, pltpu.roll(after, W2, 1)], axis=0).astype(jnp.bfloat16)
    put(total_first + jnp.dot(left, band[:EDGE, :EDGE], preferred_element_type=jnp.float32), slice(0, EDGE))
    put(
        total_last + jnp.dot(right, band[2 * EDGE : 3 * EDGE, :EDGE], preferred_element_type=jnp.float32),
        slice(length - EDGE, length),
    )

    give_pieces(1)
    give_sources(1)

    count = groups * 16
    blank = jnp.zeros((count, SLOT - length), jnp.float32)

    def place(slot, middle, ends):
        middle, ends = middle.astype(jnp.float32), ends.astype(jnp.float32)
        wide = jnp.concatenate([ends[:, :EDGE], middle, ends[:, EDGE:], blank], axis=1)
        late = pltpu.roll(wide, LATE, 1)
        two = jnp.concatenate([wide.reshape(groups, 16, SLOT), late.reshape(groups, 16, SLOT)], axis=1)
        lagged[:, slot * SLOT : slot * SLOT + SLOT] = two.reshape(groups * 32, SLOT).astype(jnp.bfloat16)

    between[0].wait_recv()
    onward[0].start()
    place(0, pieces[0, pair], pieces[1, pair])
    for copy in beside:
        copy.wait_recv()
    place(1, pieces_in[0, 0], pieces_in[1, 0])
    between[1].wait_recv()
    onward[1].start()
    place(2, pieces_in[0, 1], pieces_in[1, 1])
    n_src = REACH * SRC
    for slot in range(4):
        for kind in range(2):
            for place_o in range(REACH):
                send(
                    mine.at[0], sources_in.at[kind, slot, place_o], src_s.at[0, 0, 0],
                    src_r.at[kind, slot, place_o], chan_at(1), tm,
                ).wait_recv()
        middle, ends = [sources_in[kind, slot].astype(jnp.float32) for kind in range(2)]
        joined = jnp.concatenate(
            [ends[:, :SRC], middle[:, :SRC], middle[:, SRC:], ends[:, SRC:]], axis=2
        ).reshape(n_src, length)
        padded[:, slot * SLOT : slot * SLOT + SLOT] = jnp.concatenate(
            [joined, jnp.zeros((n_src, SLOT - length), jnp.float32)], axis=1
        )
    for copy in onward:
        copy.wait_recv()
    place(3, pieces_in[0, 2], pieces_in[1, 2])

    scale = 1.0 / float(length * n_tm) ** 0.5

    def partial_copy(chunk, delta):
        first, last = CHUNKS[chunk]
        to = lax.rem(group + delta, groups)
        part = pl.ds(first, last - first)
        return send(
            partial.at[to, part], partial_in.at[delta - 1, part],
            part_s.at[chunk, delta - 1], part_r.at[chunk, delta - 1], chan, cousin(delta),
        )

    def product(shifts):
        wide = padded[...]
        shifted = jnp.concatenate([pltpu.roll(wide, c, 1) if c else wide for c in shifts], axis=0)
        result = lax.dot_general(
            lagged[...], shifted.astype(jnp.bfloat16), (((1,), (1,)), ((), ())),
            preferred_element_type=jnp.float32,
        )
        return (result * scale).reshape(groups, 2, 16, len(shifts) * n_src)

    for step in range(4):
        if step < 3:
            result = product(range(8 * step, 8 * step + 8)).astype(jnp.bfloat16)
            for late in range(2):
                for side in range(2):
                    partial[:, 4 * step + 2 * late + side] = result[:, late, :, side * 128 : side * 128 + 128]
        else:
            result = product(range(24, 26))
            partial[:, 12] = jnp.concatenate([result[:, 0], result[:, 1]], axis=2).astype(jnp.bfloat16)
        for chunk, (first, last) in enumerate(CHUNKS):
            if last == min(4 * step + 4, TILES):
                for delta in FAR_FIRST:
                    partial_copy(chunk, delta).start()

    tall = 512
    k = lax.broadcasted_iota(jnp.int32, (tall, tall), 0)
    j = lax.broadcasted_iota(jnp.int32, (tall, tall), 1)
    b = jnp.bitwise_and(k, 7)
    tile = jnp.bitwise_and(jnp.right_shift(k, 3), 15)
    quarter = jnp.right_shift(k, 7)
    mixed = tile == 12
    late = jnp.where(mixed, jnp.right_shift(quarter, 1), jnp.bitwise_and(jnp.right_shift(tile, 1), 1))
    shift = jnp.where(
        mixed, 24 + jnp.bitwise_and(quarter, 1),
        8 * jnp.right_shift(tile, 2) + 4 * jnp.bitwise_and(tile, 1) + quarter,
    )
    lag = shift - LATE * late + MAXLAG
    fits = jnp.logical_and(jnp.logical_and(lag >= 0, tile < TILES), b * LAGS + lag == j)
    order = fits.astype(jnp.float32).astype(jnp.bfloat16)

    total = partial[group].astype(jnp.float32)
    for delta in FAR_FIRST[::-1]:
        for chunk in range(len(CHUNKS)):
            partial_copy(chunk, delta).wait_recv()
        total = total + partial_in[delta - 1].astype(jnp.float32)
    spare = jnp.zeros((24, 128), jnp.float32)
    stack = []
    for owner in range(2):
        stack += [total[:, owner * 8 : owner * 8 + 8, :].reshape(TILES * 8, 128), spare]
    turned = jnp.concatenate(stack, axis=0).T
    flat = jnp.concatenate(
        [
            jnp.concatenate(
                [turned[n_src * s : n_src * s + n_src, owner * 128 : owner * 128 + 128] for s in range(4)], axis=1
            )
            for owner in range(2)
        ],
        axis=0,
    )
    high, low = split(flat)
    moved = jnp.dot(jnp.concatenate([high, low], axis=0), order, preferred_element_type=jnp.float32)
    sums[...] = moved[: 2 * n_src] + moved[2 * n_src :]

    sum_sends = []
    for place_o in range(REACH):
        low_d, high_d = OFFSETS[place_o], OFFSETS[REACH + place_o]
        back = chan_at(-low_d - core * (high_d - low_d))
        for owner in range(2):
            o = PLACES[place_o] + core * (PLACES[REACH + place_o] - PLACES[place_o])
            sum_sends.append(
                send(
                    sums.at[pl.ds((owner * REACH + place_o) * SRC, SRC), :], stacked.at[o],
                    sum_s.at[owner, place_o], sum_r.at[o], back, group * 4 + pair * 2 + owner,
                )
            )
            sum_sends[-1].start()
    for o in range(2 * REACH):
        send(sums.at[pl.ds(0, SRC), :], stacked.at[o], sum_s.at[0, 0], sum_r.at[o], chan_at(1), tm).wait_recv()
    out_ref[...] = stacked[...]

    to_right.wait_send()
    to_left.wait_send()
    for copy in source_sends + beside + between + onward + sum_sends:
        copy.wait_send()
    for chunk in range(len(CHUNKS)):
        for delta in range(1, groups):
            partial_copy(chunk, delta).wait_send()


def body(sizes, strain_rate):
    rows, length = strain_rate.shape
    n_chan, n_tm = sizes
    groups = n_tm // 4
    n_off = len(OFFSETS)
    f32, bf16 = jnp.float32, jnp.bfloat16
    dma = pltpu.SemaphoreType.DMA
    stacks = pl.pallas_call(
        functools.partial(correlate_kernel, sizes),
        out_shape=jax.ShapeDtypeStruct((n_off, SRC, 512), f32),
        in_specs=[pl.BlockSpec(memory_space=pl.ANY)],
        out_specs=pl.BlockSpec(memory_space=pltpu.VMEM),
        scratch_shapes=[
            pltpu.VMEM((rows, length), f32),
            pltpu.VMEM((2, rows // 2, EDGE), bf16),
            pltpu.VMEM((2, rows // 2, EDGE), bf16),
            pltpu.VMEM((rows, length), f32),
            pltpu.VMEM((2, 2, rows // 2, length // 2), bf16),
            pltpu.VMEM((2, 3, rows // 2, length // 2), bf16),
            pltpu.VMEM((2, 2 * SRC, EDGE), bf16),
            pltpu.VMEM((2, 4, REACH, 2 * SRC, EDGE), bf16),
            pltpu.VMEM((groups * 32, 4 * SLOT), bf16),
            pltpu.VMEM((REACH * SRC, 4 * SLOT), f32),
            pltpu.VMEM((groups, TILES, 16, 128), bf16),
            pltpu.VMEM((groups - 1, TILES, 16, 128), bf16),
            pltpu.VMEM((2 * REACH * SRC, 512), f32),
            pltpu.VMEM((n_off, SRC, 512), f32),
            dma, pltpu.SemaphoreType.REGULAR, dma((2,)), dma((2,)), dma((6,)), dma((6,)),
            dma((2, 2, n_off)), dma((2, 4, REACH)),
            dma((len(CHUNKS), groups - 1)), dma((len(CHUNKS), groups - 1)),
            dma((2, REACH)), dma((n_off,)),
        ],
        compiler_params=pltpu.CompilerParams(
            collective_id=0, has_side_effects=True, vmem_limit_bytes=55000 * 1024
        ),
    )(strain_rate)
    return jnp.transpose(stacks[:, :, : (rows // n_tm) * LAGS], (1, 0, 2))


def solution(mesh):
    sizes = (mesh.shape["chan"], mesh.shape["tm"])
    return jax.shard_map(
        functools.partial(body, sizes), mesh=mesh, in_specs=(P("chan", "tm"),),
        out_specs=P("chan", None, "tm"), check_vma=False,
    )
```
